32 devices in a mesh: parts: 2 (over y), ctx: 4 (over z), grid: 4 (over x, core).
Axes of the slice: x: 2, y: 2, z: 4, core: 2. Of those that a mesh axis runs over, the one named last changes fastest.
Arguments:
- frames_in: bfloat16 [4096, 1536], P(('parts', 'ctx'), 'grid'), parts along dimension 0, may hold values from -230 to 230
- norm1_gain: bfloat16 [1536], P('grid'), may hold values from 0.25 to 1.75
- norm1_bias: bfloat16 [1536], P('grid'), may hold values from -3 to 3
- w_query: bfloat16 [1536, 1536], P(None, 'grid'), may hold values from -0.5 to 0.5
- w_key: bfloat16 [1536, 1536], P(None, 'grid'), may hold values from -2 to 2
- w_value: bfloat16 [1536, 1536], P(None, 'grid'), may hold values from -0.15625 to 0.15625
- w_out: bfloat16 [1536, 1536], P('grid'), may hold values from -0.15625 to 0.15625
- norm2_gain: bfloat16 [1536], P('grid'), may hold values from 0.099609375 to 1.8984375
- norm2_bias: bfloat16 [1536], P('grid'), may hold values from -3 to 3
- w_glu_value: bfloat16 [1536, 1536], P(None, 'grid'), may hold values from -0.15625 to 0.15625
- w_glu_gate: bfloat16 [1536, 1536], P(None, 'grid'), may hold values from -0.15625 to 0.15625
- depth_kernel: float32 [31, 1536], P(None, 'grid'), may hold values from -1 to 1
- bn_scale: float32 [1536], P('grid'), may hold values from 0.25 to 1.75
- bn_shift: float32 [1536], P('grid'), may hold values from -3 to 3
- w_proj: bfloat16 [1536, 1536], P('grid'), may hold values from -0.3125 to 0.3125
Outputs:
- layer_out: bfloat16 [4096, 1536], P(('parts', 'ctx'), 'grid'), parts along dimension 0
The draws below stay inside these ranges and needn't reach their ends.
There are 2 independent parts, one for each index of `parts`. The reference program is written for one: setup_inputs(seed, part) draws one part's arguments, and reference() takes and returns one part's arrays. A program takes and returns all parts, laid end to end along the dimension named above; an argument that names none is the same for every part. Nothing has to cross between parts.
All inputs are finite; a program needn't handle non-finite values.
Results may differ from the reference program's by a relative error of at most 0.009.
Values may be sent and summed in bfloat16 or wider, within the bound.
A program may use at most 256 MiB of HBM per device.

```python
import math
import jax
import jax.numpy as jnp
from jax import lax

D = 1536
HEADS = 24
HEAD_DIM = 64
KERNEL = 31
HALF = 15
FRAMES = 2048
N_GRID = 4


def draw_frames_in(key, part):
    first_key = jax.random.fold_in(key, 0)
    columns = jnp.arange(D, dtype=jnp.float32)
    column_scale = jnp.exp(math.log(10.0) * columns / (D - 1))
    base = jnp.clip(jax.random.normal(first_key, (FRAMES, D), jnp.float32), -4.0, 4.0)
    result = base * column_scale
    return result.astype(jnp.bfloat16)


def query_key_base(key):
    base_key = jax.random.fold_in(key, 101)
    first_key, second_key = jax.random.split(base_key, 2)
    first_normal = jnp.clip(jax.random.normal(first_key, (D, D), jnp.float32), -6.0, 6.0)
    second_normal = jnp.clip(jax.random.normal(second_key, (D, D), jnp.float32), -6.0, 6.0)
    return (first_normal, second_normal)


def draw_w_query(key, part):
    first_normal, second_normal = query_key_base(key)
    return jnp.clip(3.0 * first_normal / math.sqrt(D), -0.5, 0.5).astype(jnp.bfloat16)


def draw_w_key(key, part):
    first_normal, second_normal = query_key_base(key)
    result = second_normal / math.sqrt(D)
    return jnp.clip(result, -2.0, 2.0).astype(jnp.bfloat16)


def steps_of(key, extent, pieces, low, high):
    level, own = 1.0, jax.random.fold_in(key, 6)
    for dim, parts in pieces:
        draws = jnp.exp(jax.random.uniform(jax.random.fold_in(own, dim), (parts,), jnp.float32, low / len(pieces), high / len(pieces)))
        level = level * jnp.repeat(draws, extent[dim] // parts).reshape([-1 if axis == dim else 1 for axis in range(len(extent))])
    return level


def centred(rng, dims, width, limit, cuts=(), held_as=jnp.bfloat16):
    drawn = width * jax.random.normal(rng, dims, jnp.float32)
    if cuts:
        drawn = drawn * steps_of(rng, dims, cuts, -0.22, 0.18)
    return jnp.clip(drawn, -limit, limit).astype(held_as)


def setup_inputs(seed: int = 0, part: int = 0) -> dict:
    key_list = jax.random.split(jax.random.key(seed), 16)
    own_keys = jax.random.split(jax.random.fold_in(key_list[15], part), 16)
    frames_in = draw_frames_in(jax.random.fold_in(jax.random.fold_in(key_list[15], part), 71), part)
    norm1_gain = jnp.clip(1.0 + 0.15 * jax.random.normal(key_list[1], (D,), jnp.float32), 0.25, 1.75).astype(jnp.bfloat16)
    norm1_bias = centred(key_list[2], (D,), 0.5, 3.0, ((0, 4),))
    w_query = draw_w_query(jax.random.fold_in(key_list[15], 71), part)
    w_key = draw_w_key(jax.random.fold_in(key_list[15], 71), part)
    w_value = centred(key_list[5], (D, D), D ** -0.5, 0.15625, ((1, 4),))
    w_out = centred(key_list[6], (D, D), D ** -0.5, 0.15625, ((0, 4),))
    norm2_gain = jnp.clip(1.0 + 0.18 * jax.random.normal(key_list[7], (D,), jnp.float32), 0.099609375, 1.8984375).astype(jnp.bfloat16)
    norm2_bias = centred(key_list[8], (D,), 0.5, 3.0, ((0, 4),))
    w_glu_value = centred(key_list[9], (D, D), D ** -0.5, 0.15625, ((1, 4),))
    w_glu_gate = centred(key_list[10], (D, D), D ** -0.5, 0.15625, ((1, 4),))
    depth_kernel = centred(key_list[11], (KERNEL, D), KERNEL ** -0.5, 1.0, ((1, 4),), jnp.float32)
    bn_scale = jnp.clip(1.0 + 0.15 * jax.random.normal(key_list[12], (D,), jnp.float32), 0.25, 1.75)
    bn_shift = centred(key_list[13], (D,), 0.5, 3.0, ((0, 4),), jnp.float32)
    w_proj = centred(key_list[14], (D, D), (D // 4) ** -0.5, 0.3125, ((0, 4),))
    return dict(frames_in=frames_in, norm1_gain=norm1_gain, norm1_bias=norm1_bias, w_query=w_query, w_key=w_key, w_value=w_value, w_out=w_out, norm2_gain=norm2_gain, norm2_bias=norm2_bias, w_glu_value=w_glu_value, w_glu_gate=w_glu_gate, depth_kernel=depth_kernel, bn_scale=bn_scale, bn_shift=bn_shift, w_proj=w_proj)


EPSILON = 1e-05

def layer_norm(values, gain_vec, shift_vec):
    values = values.astype(jnp.float32)
    row_mean = lax.optimization_barrier(jnp.mean(values, axis=1, keepdims=True))
    variance = lax.optimization_barrier(jnp.mean(jnp.square(values - row_mean), axis=1, keepdims=True))
    scaled = (values - row_mean) * lax.rsqrt(variance + EPSILON)
    return (scaled * gain_vec.astype(jnp.float32) + shift_vec.astype(jnp.float32)).astype(jnp.bfloat16)

def grouped_product(activation, weight):
    group_width = activation.shape[1] // N_GRID
    running = jnp.zeros((activation.shape[0], weight.shape[1]), jnp.float32)
    for group_index in range(N_GRID):
        lower = group_index * group_width
        partial_sum = jnp.dot(activation[:, lower:lower + group_width], weight[lower:lower + group_width], preferred_element_type=jnp.float32)
        rounded = lax.optimization_barrier(partial_sum.astype(jnp.bfloat16))
        running = running + rounded.astype(jnp.float32)
    return running

def attend_all(queries, key_rows, value_rows):
    frame_count = queries.shape[0]
    block_rows = math.gcd(frame_count, 512)
    key_heads = key_rows.reshape(frame_count, HEADS, HEAD_DIM).astype(jnp.float32)
    value_heads = value_rows.reshape(frame_count, HEADS, HEAD_DIM).astype(jnp.float32)

    def one_block(query_block):
        query_heads = query_block.reshape(block_rows, HEADS, HEAD_DIM).astype(jnp.float32)
        scores = jnp.einsum('qhd,khd->hqk', query_heads, key_heads) * (1.0 / math.sqrt(HEAD_DIM))
        peak = lax.optimization_barrier(jnp.max(scores, axis=2, keepdims=True))
        soft = jnp.exp(scores - peak)
        totals = lax.optimization_barrier(jnp.sum(soft, axis=2))
        soft_rounded = lax.optimization_barrier(soft.astype(jnp.bfloat16))
        mixed = jnp.einsum('hqk,khd->qhd', soft_rounded.astype(jnp.float32), value_heads)
        mixed = mixed / jnp.transpose(totals)[:, :, None]
        return mixed.reshape(block_rows, HEADS * HEAD_DIM).astype(jnp.bfloat16)
    blocks = queries.reshape(frame_count // block_rows, block_rows, HEADS * HEAD_DIM)
    return lax.map(one_block, blocks).reshape(frame_count, HEADS * HEAD_DIM)

def reference(frames_in, norm1_gain, norm1_bias, w_query, w_key, w_value, w_out, norm2_gain, norm2_bias, w_glu_value, w_glu_gate, depth_kernel, bn_scale, bn_shift, w_proj):
    normed = layer_norm(frames_in, norm1_gain, norm1_bias)
    queries = jnp.dot(normed, w_query, preferred_element_type=jnp.float32).astype(jnp.bfloat16)
    key_rows = jnp.dot(normed, w_key, preferred_element_type=jnp.float32).astype(jnp.bfloat16)
    value_rows = jnp.dot(normed, w_value, preferred_element_type=jnp.float32).astype(jnp.bfloat16)
    attended = attend_all(queries, key_rows, value_rows)
    middle = (frames_in.astype(jnp.float32) + grouped_product(attended, w_out)).astype(jnp.bfloat16)
    normed_conv = layer_norm(middle, norm2_gain, norm2_bias)
    value_part = jnp.dot(normed_conv, w_glu_value, preferred_element_type=jnp.float32)
    gate_part = jnp.dot(normed_conv, w_glu_gate, preferred_element_type=jnp.float32)
    gated = lax.optimization_barrier((value_part * jax.nn.sigmoid(gate_part)).astype(jnp.bfloat16))
    padded = jnp.pad(gated.astype(jnp.float32), ((HALF, HALF), (0, 0)))
    frame_count = frames_in.shape[0]
    convolved = jnp.zeros((frame_count, frames_in.shape[1]), jnp.float32)
    for tap_index in range(KERNEL):
        convolved = convolved + depth_kernel[tap_index] * padded[tap_index:tap_index + frame_count]
    activated = jax.nn.silu(convolved * bn_scale + bn_shift).astype(jnp.bfloat16)
    return (middle.astype(jnp.float32) + grouped_product(activated, w_proj)).astype(jnp.bfloat16)
```

```python
import math

import jax
import jax.numpy as jnp
from jax import lax
from jax.experimental import pallas as pl
from jax.experimental.pallas import tpu as pltpu
from jax.sharding import PartitionSpec as P

HEAD_DIM = 64
KERNEL = 31
HALF = 15
EPSILON = 1e-05
LANES = 128
PAD = 16
MESH = pl.DeviceIdType.MESH
F32 = jnp.float32
BF16 = jnp.bfloat16
VMEM_LIMIT = 56 * 1024 * 1024


def remote(src, dst, send, recv, axis, index):
    return pltpu.make_async_remote_copy(
        src_ref=src,
        dst_ref=dst,
        send_sem=send,
        recv_sem=recv,
        device_id={axis: index},
        device_id_type=MESH,
    )


class GridGather:
    def __init__(self, size, sems):
        self.me = lax.axis_index("grid")
        self.chips = size // 2
        self.chip = self.me // 2
        self.core = self.me % 2
        self.mate = self.chip * 2 + 1 - self.core
        self.sems = sems

    def peer(self, step):
        return lax.rem(self.chip + step, self.chips) * 2 + self.core

    def source(self, step):
        return lax.rem(self.chip + self.chips - step, self.chips) * 2 + self.core

    def source_mate(self, step):
        return lax.rem(self.chip + self.chips - step, self.chips) * 2 + 1 - self.core

    def greet(self, barrier):
        pl.semaphore_signal(barrier, inc=1, device_id={"grid": self.mate}, device_id_type=MESH)
        for step in range(1, self.chips):
            pl.semaphore_signal(
                barrier, inc=1, device_id={"grid": self.peer(step)}, device_id_type=MESH
            )
        return self.chips

    def own(self, view, part, step):
        ref = view(self.me)
        target = self.mate if step == 0 else self.peer(step)
        return remote(ref, ref, self.sems.at[0, step, part], self.sems.at[1, step, part], "grid", target)

    def arrived(self, view, part, step):
        slot = self.mate if step == 0 else self.source(step)
        ref = view(slot)
        return remote(ref, ref, self.sems.at[0, step, part], self.sems.at[1, step, part], "grid", self.mate)

    def relay(self, view, part, step):
        ref = view(self.source(step))
        return remote(ref, ref, self.sems.at[2, step, part], self.sems.at[3, step, part], "grid", self.mate)

    def relayed(self, view, part, step):
        ref = view(self.source_mate(step))
        return remote(ref, ref, self.sems.at[2, step, part], self.sems.at[3, step, part], "grid", self.mate)

    def start(self, view, part):
        for step in range(1, self.chips):
            self.own(view, part, step).start()
        self.own(view, part, 0).start()

    def forward(self, view, part):
        for step in range(1, self.chips):
            self.arrived(view, part, step).wait_recv()
            self.relay(view, part, step).start()

    def finish(self, view, part):
        self.arrived(view, part, 0).wait_recv()
        for step in range(1, self.chips):
            self.relayed(view, part, step).wait_recv()

    def drain(self, view, part):
        for step in range(self.chips):
            self.own(view, part, step).wait_send()
        for step in range(1, self.chips):
            self.relay(view, part, step).wait_send()


def gather_sems(size, parts):
    return pltpu.SemaphoreType.DMA((4, size // 2, parts))


def normalize(pieces, gains, shifts):
    width = pieces[0].shape[1] * len(pieces)
    total = sum(jnp.sum(piece, axis=1, keepdims=True) for piece in pieces)
    mean = total / width
    centred = [piece - mean for piece in pieces]
    square = sum(jnp.sum(piece * piece, axis=1, keepdims=True) for piece in centred)
    scale = lax.rsqrt(square / width + EPSILON)
    return [
        (piece * scale * gain + shift).astype(BF16)
        for piece, gain, shift in zip(centred, gains, shifts)
    ]


def project(pieces, weight_ref):
    width = pieces[0].shape[1]
    total = None
    for index, piece in enumerate(pieces):
        term = jnp.dot(
            piece, weight_ref[index * width : (index + 1) * width, :], preferred_element_type=F32
        )
        total = term if total is None else total + term
    return total


def first_kernel(
    size, parts, x_ref, affine_ref, wq_hbm, wk_hbm, wv_hbm,
    xg_ref, affg_ref, q_ref, kv_ref,
    wq_ref, wk_ref, wv_ref, sems, aff_sems, load_sems,
):
    rows = x_ref.shape[0]
    step_rows = rows // parts
    gather = GridGather(size, sems)
    small = GridGather(size, aff_sems)
    loads = [
        pltpu.make_async_copy(src, dst, load_sems.at[index])
        for index, (src, dst) in enumerate(((wq_hbm, wq_ref), (wk_hbm, wk_ref), (wv_hbm, wv_ref)))
    ]
    for load in loads:
        load.start()
    barrier = pltpu.get_barrier_semaphore()
    count = gather.greet(barrier)
    xg_ref[gather.me] = x_ref[...]
    affg_ref[gather.me] = affine_ref[...]
    pl.semaphore_wait(barrier, count)

    def view(part):
        return lambda slot: xg_ref.at[slot, pl.ds(part * step_rows, step_rows), :]

    def small_view(slot):
        return affg_ref.at[slot]

    small.start(small_view, 0)
    for part in range(parts):
        gather.start(view(part), part)
    small.forward(small_view, 0)
    gather.forward(view(0), 0)
    small.finish(small_view, 0)
    for load in loads:
        load.wait()
    gains = [affg_ref[index, 0:1, :] for index in range(size)]
    shifts = [affg_ref[index, 1:2, :] for index in range(size)]
    scale = math.log2(math.e) / math.sqrt(HEAD_DIM)
    for part in range(parts):
        if part + 1 < parts:
            gather.forward(view(part + 1), part + 1)
        gather.finish(view(part), part)
        span = slice(part * step_rows, (part + 1) * step_rows)
        pieces = [xg_ref[index, span, :].astype(F32) for index in range(size)]
        normed = normalize(pieces, gains, shifts)
        q_ref[span, :] = (project(normed, wq_ref) * scale).astype(BF16)
        kv_ref[0, span, :] = project(normed, wk_ref).astype(BF16)
        kv_ref[1, span, :] = project(normed, wv_ref).astype(BF16)
    small.drain(small_view, 0)
    for part in range(parts):
        gather.drain(view(part), part)


def attend_kernel(
    size, count, parts, q_ref, kv_ref, wo_ref, wp_ref,
    att_ref, wog_ref, wpg_ref,
    kvg_ref, qm_ref, max_ref, acc_ref, right_sems, left_sems, wo_sems, wp_sems, load_sems,
):
    rows, width = q_ref.shape
    heads = width // HEAD_DIM
    step_rows = rows // parts
    ctx = lax.axis_index("ctx")
    gather = GridGather(size, wo_sems)
    me = gather.me
    has_left = ctx > 0
    has_right = ctx < count - 1
    barrier = pltpu.get_barrier_semaphore()
    for step in range(1, size):
        pl.semaphore_signal(
            barrier, inc=1, device_id={"grid": lax.rem(me + step, size)}, device_id_type=MESH
        )

    @pl.when(has_left)
    def _():
        pl.semaphore_signal(barrier, inc=1, device_id={"ctx": ctx - 1}, device_id_type=MESH)

    @pl.when(has_right)
    def _():
        pl.semaphore_signal(barrier, inc=1, device_id={"ctx": ctx + 1}, device_id_type=MESH)

    kvg_ref[ctx] = kv_ref[...]
    inner = (ctx + count - 1) // count + (2 * count - 2 - ctx) // count
    pl.semaphore_wait(barrier, size - 1 + inner)

    def block(slot, part):
        return kvg_ref.at[slot, :, pl.ds(part * step_rows, step_rows), :]

    def to_right(step, part):
        ref = block(ctx - step, part)
        return remote(ref, ref, right_sems.at[0, step, part], right_sems.at[1, step, part], "ctx", ctx + 1)

    def from_left(step, part):
        ref = block(ctx - 1 - step, part)
        return remote(ref, ref, right_sems.at[0, step, part], right_sems.at[1, step, part], "ctx", ctx - 1)

    def to_left(step, part):
        ref = block(ctx + step, part)
        return remote(ref, ref, left_sems.at[0, step, part], left_sems.at[1, step, part], "ctx", ctx - 1)

    def from_right(step, part):
        ref = block(ctx + 1 + step, part)
        return remote(ref, ref, left_sems.at[0, step, part], left_sems.at[1, step, part], "ctx", ctx + 1)

    for part in range(parts):

        @pl.when(has_right)
        def _():
            to_right(0, part).start()

        @pl.when(has_left)
        def _():
            to_left(0, part).start()

    def wo_view(slot):
        return wog_ref.at[slot]

    for step in range(gather.chips):
        target = gather.mate if step == 0 else gather.peer(step)
        remote(wo_ref, wog_ref.at[me], wo_sems.at[0, step, 0], wo_sems.at[1, step, 0], "grid", target).start()

    def send_wp(step):
        target = lax.rem(me + step, size)
        return remote(wp_ref.at[target], wpg_ref.at[me], wp_sems.at[0, step], wp_sems.at[1, step], "grid", target)

    for step in range(1, size):
        send_wp(step).start()
    loads = [
        pltpu.make_async_copy(wo_ref, wog_ref.at[me], load_sems.at[0]),
        pltpu.make_async_copy(wp_ref.at[me], wpg_ref.at[me], load_sems.at[1]),
    ]
    for load in loads:
        load.start()

    spans = []
    for head in range(heads):
        low = head * HEAD_DIM // LANES * LANES
        high = min(low + LANES, width)
        spans.append((low, high))
        pair = q_ref[:, low:high]
        lane = lax.broadcasted_iota(jnp.int32, pair.shape, 1)
        inside = lane // HEAD_DIM == (head * HEAD_DIM - low) // HEAD_DIM
        qm_ref[head, :, 0 : high - low] = jnp.where(inside, pair, jnp.zeros_like(pair))

    def attend(slot, first):
        for head in range(heads):
            low, high = spans[head]
            keys = kvg_ref[slot, 0, :, low:high]
            values = kvg_ref[slot, 1, :, low:high]
            extra = [jnp.ones((rows, LANES), BF16)]
            if high - low < LANES:
                extra = [jnp.zeros((rows, LANES - (high - low)), BF16)] + extra
            values = jnp.concatenate([values] + extra, axis=1)
            scores = lax.dot_general(
                qm_ref[head, :, 0 : high - low], keys, (((1,), (1,)), ((), ())),
                preferred_element_type=F32,
            )
            peak = jnp.max(scores, axis=1, keepdims=True)
            if first:
                peak = jnp.broadcast_to(peak, (rows, LANES))
                soft = jnp.exp2(scores - jnp.concatenate([peak] * (rows // LANES), axis=1)).astype(BF16)
                acc_ref[head] = jnp.dot(soft, values, preferred_element_type=F32)
            else:
                old = max_ref[head]
                peak = jnp.maximum(old, peak)
                factor = jnp.exp2(old - peak)
                soft = jnp.exp2(scores - jnp.concatenate([peak] * (rows // LANES), axis=1)).astype(BF16)
                acc_ref[head] = acc_ref[head] * jnp.concatenate([factor, factor], axis=1) + jnp.dot(
                    soft, values, preferred_element_type=F32
                )
            max_ref[head] = peak

    attend(ctx, True)

    @pl.loop(0, count - 1)
    def _(step):
        left_there = ctx - 1 - step >= 0
        right_there = ctx + 1 + step <= count - 1
        for part in range(parts):

            @pl.when(left_there)
            def _():
                from_left(step, part).wait_recv()

                @pl.when(has_right)
                def _():
                    to_right(step + 1, part).start()

            @pl.when(right_there)
            def _():
                from_right(step, part).wait_recv()

                @pl.when(has_left)
                def _():
                    to_left(step + 1, part).start()

        @pl.when(step == count - 2)
        def _():
            gather.forward(wo_view, 0)

        @pl.loop(0, 2)
        def _(side):
            slot = jnp.where(side == 0, ctx - 1 - step, ctx + 1 + step)

            @pl.when((slot >= 0) & (slot <= count - 1))
            def _():
                attend(slot, False)

    for pair in range((heads + 1) // 2):
        low, high = spans[2 * pair]
        results = [
            acc_ref[head, :, 0:LANES] / acc_ref[head, :, LANES : 2 * LANES]
            for head in range(2 * pair, min(2 * pair + 2, heads))
        ]
        if len(results) == 2:
            lane = lax.broadcasted_iota(jnp.int32, (rows, LANES), 1)
            mixed = jnp.where(lane < HEAD_DIM, results[0], results[1])
        else:
            mixed = results[0]
        att_ref[:, low:high] = mixed[:, 0 : high - low].astype(BF16)

    gather.finish(wo_view, 0)
    for step in range(gather.chips):
        target = gather.mate if step == 0 else gather.peer(step)
        remote(wo_ref, wog_ref.at[me], wo_sems.at[0, step, 0], wo_sems.at[1, step, 0], "grid", target).wait_send()
    for step in range(1, gather.chips):
        gather.relay(wo_view, 0, step).wait_send()
    for step in range(1, size):
        send_wp(step).wait_send()
        source = lax.rem(me + size - step, size)
        remote(wp_ref.at[me], wpg_ref.at[source], wp_sems.at[0, step], wp_sems.at[1, step], "grid", source).wait_recv()
    for load in loads:
        load.wait()

    @pl.loop(0, count - 1)
    def _(step):
        for part in range(parts):

            @pl.when(has_right & (ctx - step >= 0))
            def _():
                to_right(step, part).wait_send()

            @pl.when(has_left & (ctx + step <= count - 1))
            def _():
                to_left(step, part).wait_send()


def last_kernel(
    size, count, parts, att_ref, xg_ref, affg_ref, wog_hbm, wgv_hbm, wgg_hbm, wpg_hbm,
    taps_ref, bn_ref, out_ref,
    attg_ref, actg_ref, mid_ref, gated_ref, wo_ref, wgv_ref, wgg_ref, wp_ref,
    att_sems, act_sems, halo_sems, load_sems,
):
    rows, width = att_ref.shape
    step_rows = rows // parts
    ctx = lax.axis_index("ctx")
    attended = GridGather(size, att_sems)
    activated = GridGather(size, act_sems)
    me = attended.me
    has_left = ctx > 0
    has_right = ctx < count - 1
    loads = [
        pltpu.make_async_copy(src, dst, load_sems.at[index])
        for index, (src, dst) in enumerate(
            ((wog_hbm, wo_ref), (wgv_hbm, wgv_ref), (wgg_hbm, wgg_ref), (wpg_hbm, wp_ref))
        )
    ]
    for load in loads:
        load.start()
    barrier = pltpu.get_barrier_semaphore()
    greeted = attended.greet(barrier)

    @pl.when(has_left)
    def _():
        pl.semaphore_signal(barrier, inc=1, device_id={"ctx": ctx - 1}, device_id_type=MESH)

    @pl.when(has_right)
    def _():
        pl.semaphore_signal(barrier, inc=1, device_id={"ctx": ctx + 1}, device_id_type=MESH)

    attg_ref[me] = att_ref[...]
    inner = (ctx + count - 1) // count + (2 * count - 2 - ctx) // count
    pl.semaphore_wait(barrier, greeted + inner)

    def view(buffer, part):
        return lambda slot: buffer.at[slot, pl.ds(part * step_rows, step_rows), :]

    for part in range(parts):
        attended.start(view(attg_ref, part), part)

    @pl.when(jnp.logical_not(has_left))
    def _():
        gated_ref[0:PAD, :] = jnp.zeros((PAD, width), F32)

    @pl.when(jnp.logical_not(has_right))
    def _():
        gated_ref[PAD + rows : 2 * PAD + rows, :] = jnp.zeros((PAD, width), F32)

    def halo_left(index):
        return remote(
            gated_ref.at[PAD : 2 * PAD, :], gated_ref.at[PAD + rows : 2 * PAD + rows, :],
            halo_sems.at[0], halo_sems.at[1], "ctx", index,
        )

    def halo_right(index):
        return remote(
            gated_ref.at[rows : rows + PAD, :], gated_ref.at[0:PAD, :],
            halo_sems.at[2], halo_sems.at[3], "ctx", index,
        )

    attended.forward(view(attg_ref, 0), 0)
    for load in loads:
        load.wait()
    gains = [affg_ref[index, 2:3, :] for index in range(size)]
    shifts = [affg_ref[index, 3:4, :] for index in range(size)]
    for part in range(parts):
        if part + 1 < parts:
            attended.forward(view(attg_ref, part + 1), part + 1)
        attended.finish(view(attg_ref, part), part)
        span = slice(part * step_rows, (part + 1) * step_rows)
        sources = [attg_ref[index, span, :] for index in range(size)]
        pieces = []
        for column in range(size):
            total = xg_ref[column, span, :].astype(F32)
            for index in range(size):
                total = total + jnp.dot(
                    sources[index], wo_ref[index, column], preferred_element_type=F32
                )
            middle = total.astype(BF16)
            mid_ref[column, span, :] = middle
            pieces.append(middle.astype(F32))
        normed = normalize(pieces, gains, shifts)
        gate = project(normed, wgg_ref)
        value = project(normed, wgv_ref)
        gated = (value * (1.0 / (1.0 + jnp.exp(-gate)))).astype(BF16)
        gated_ref[PAD + part * step_rows : PAD + (part + 1) * step_rows, :] = gated.astype(F32)
        if part == 0:

            @pl.when(has_left)
            def _():
                halo_left(ctx - 1).start()

    @pl.when(has_right)
    def _():
        halo_right(ctx + 1).start()

    block_rows = min(32, step_rows)
    inner_parts = list(range(1, parts - 1))
    for order, part in enumerate(inner_parts + [0] + ([parts - 1] if parts > 1 else [])):
        if order == len(inner_parts):

            @pl.when(has_left)
            def _():
                halo_right(ctx - 1).wait_recv()

            @pl.when(has_right)
            def _():
                halo_left(ctx + 1).wait_recv()

        @pl.loop(0, step_rows // block_rows)
        def _(block):
            base = pl.multiple_of(part * step_rows + block * block_rows, block_rows)
            window = gated_ref[pl.ds(base, block_rows + 2 * PAD), :]
            total = jnp.zeros((block_rows, width), F32)
            for tap in range(KERNEL):
                low = tap + PAD - HALF
                total = total + taps_ref[tap : tap + 1, :] * window[low : low + block_rows, :]
            scaled = total * bn_ref[0:1, :] + bn_ref[1:2, :]
            result = scaled / (1.0 + jnp.exp(-scaled))
            actg_ref[me, pl.ds(base, block_rows), :] = result.astype(BF16)

        activated.start(view(actg_ref, part), part)

    sequence = inner_parts + [0] + ([parts - 1] if parts > 1 else [])
    activated.forward(view(actg_ref, sequence[0]), sequence[0])
    for order, part in enumerate(sequence):
        if order + 1 < parts:
            activated.forward(view(actg_ref, sequence[order + 1]), sequence[order + 1])
        activated.finish(view(actg_ref, part), part)
        span = slice(part * step_rows, (part + 1) * step_rows)
        total = mid_ref[me, span, :].astype(F32)
        for index in range(size):
            total = total + jnp.dot(
                actg_ref[index, span, :], wp_ref[index], preferred_element_type=F32
            )
        out_ref[span, :] = total.astype(BF16)

    for part in range(parts):
        attended.drain(view(attg_ref, part), part)
        activated.drain(view(actg_ref, part), part)

    @pl.when(has_left)
    def _():
        halo_left(ctx - 1).wait_send()

    @pl.when(has_right)
    def _():
        halo_right(ctx + 1).wait_send()


def params(number):
    return pltpu.CompilerParams(
        collective_id=number, has_side_effects=True, vmem_limit_bytes=VMEM_LIMIT
    )


def on_device(
    frames_in,
    norm1_gain,
    norm1_bias,
    w_query,
    w_key,
    w_value,
    w_out,
    norm2_gain,
    norm2_bias,
    w_glu_value,
    w_glu_gate,
    depth_kernel,
    bn_scale,
    bn_shift,
    w_proj,
):
    size = lax.axis_size("grid")
    count = lax.axis_size("ctx")
    rows, width = frames_in.shape
    full = width * size
    heads = width // HEAD_DIM
    vmem = pl.BlockSpec(memory_space=pltpu.VMEM)
    anywhere = pl.BlockSpec(memory_space=pl.ANY)
    dma = pltpu.SemaphoreType.DMA
    parts = 4

    def shape(dims, dtype=BF16):
        return jax.ShapeDtypeStruct(dims, dtype)

    affine = jnp.stack([norm1_gain, norm1_bias, norm2_gain, norm2_bias]).astype(F32)
    affine = jnp.pad(affine, ((0, 4), (0, 0)))
    wo_blocks = jnp.transpose(w_out.reshape(width, size, width), (1, 0, 2))
    wp_blocks = jnp.transpose(w_proj.reshape(width, size, width), (1, 0, 2))

    xg, affg, queries, key_values = pl.pallas_call(
        lambda *refs: first_kernel(size, parts, *refs),
        out_shape=(
            shape((size, rows, width)),
            shape((size, 8, width), F32),
            shape((rows, width)),
            shape((2, rows, width)),
        ),
        in_specs=[vmem, vmem, anywhere, anywhere, anywhere],
        out_specs=(vmem,) * 4,
        scratch_shapes=[pltpu.VMEM((full, width), BF16)] * 3
        + [gather_sems(size, parts), gather_sems(size, 1), dma((3,))],
        compiler_params=params(0),
        name="gather_project",
    )(frames_in, affine, w_query, w_key, w_value)

    kv_parts = 2
    attended, wo_all, wp_all = pl.pallas_call(
        lambda *refs: attend_kernel(size, count, kv_parts, *refs),
        out_shape=(
            shape((rows, width)),
            shape((size, size, width, width)),
            shape((size, width, width)),
        ),
        in_specs=[vmem, vmem, anywhere, anywhere],
        out_specs=(vmem, anywhere, anywhere),
        scratch_shapes=[
            pltpu.VMEM((count, 2, rows, width), BF16),
            pltpu.VMEM((heads, rows, LANES), BF16),
            pltpu.VMEM((heads, rows, LANES), F32),
            pltpu.VMEM((heads, rows, 2 * LANES), F32),
            dma((2, count, kv_parts)),
            dma((2, count, kv_parts)),
            gather_sems(size, 1),
            dma((2, size)),
            dma((2,)),
        ],
        compiler_params=params(1),
        name="attend_ring",
    )(queries, key_values, wo_blocks, wp_blocks)

    norms = jnp.stack([bn_scale, bn_shift])
    return pl.pallas_call(
        lambda *refs: last_kernel(size, count, parts, *refs),
        out_shape=shape((rows, width)),
        in_specs=[vmem, vmem, vmem] + [anywhere] * 4 + [vmem, vmem],
        out_specs=vmem,
        scratch_shapes=[
            pltpu.VMEM((size, rows, width), BF16),
            pltpu.VMEM((size, rows, width), BF16),
            pltpu.VMEM((size, rows, width), BF16),
            pltpu.VMEM((rows + 2 * PAD, width), F32),
            pltpu.VMEM((size, size, width, width), BF16),
            pltpu.VMEM((full, width), BF16),
            pltpu.VMEM((full, width), BF16),
            pltpu.VMEM((size, width, width), BF16),
            gather_sems(size, parts),
            gather_sems(size, parts),
            dma((4,)),
            dma((4,)),
        ],
        compiler_params=params(2),
        name="convolve_project",
    )(attended, xg, affg, wo_all, w_glu_value, w_glu_gate, wp_all, depth_kernel, norms)


def solution(mesh):
    return jax.shard_map(
        on_device,
        mesh=mesh,
        in_specs=(
            P(("parts", "ctx"), "grid"),
            P("grid"),
            P("grid"),
            P(None, "grid"),
            P(None, "grid"),
            P(None, "grid"),
            P("grid", None),
            P("grid"),
            P("grid"),
            P(None, "grid"),
            P(None, "grid"),
            P(None, "grid"),
            P("grid"),
            P("grid"),
            P("grid", None),
        ),
        out_specs=P(("parts", "ctx"), "grid"),
        check_vma=False,
    )
```

```python
import math

import jax
import jax.numpy as jnp
from jax import lax
from jax.experimental import pallas as pl
from jax.experimental.pallas import tpu as pltpu
from jax.sharding import PartitionSpec as P

HEAD_DIM = 64
KERNEL = 31
HALF = 15
EPSILON = 1e-05
LANES = 128
PAD = 16
MESH = pl.DeviceIdType.MESH
F32 = jnp.float32
BF16 = jnp.bfloat16
VMEM_LIMIT = 56 * 1024 * 1024


def remote(src, dst, send, recv, axis, index):
    return pltpu.make_async_remote_copy(
        src_ref=src,
        dst_ref=dst,
        send_sem=send,
        recv_sem=recv,
        device_id={axis: index},
        device_id_type=MESH,
    )


class GridGather:
    def __init__(self, size, sems):
        self.me = lax.axis_index("grid")
        self.chips = size // 2
        self.chip = self.me // 2
        self.core = self.me % 2
        self.mate = self.chip * 2 + 1 - self.core
        self.sems = sems

    def peer(self, step):
        return lax.rem(self.chip + step, self.chips) * 2 + self.core

    def source(self, step):
        return lax.rem(self.chip + self.chips - step, self.chips) * 2 + self.core

    def source_mate(self, step):
        return lax.rem(self.chip + self.chips - step, self.chips) * 2 + 1 - self.core

    def greet(self, barrier):
        pl.semaphore_signal(barrier, inc=1, device_id={"grid": self.mate}, device_id_type=MESH)
        for step in range(1, self.chips):
            pl.semaphore_signal(
                barrier, inc=1, device_id={"grid": self.peer(step)}, device_id_type=MESH
            )
        return self.chips

    def own(self, view, part, step):
        ref = view(self.me)
        target = self.mate if step == 0 else self.peer(step)
        return remote(ref, ref, self.sems.at[0, step, part], self.sems.at[1, step, part], "grid", target)

    def arrived(self, view, part, step):
        slot = self.mate if step == 0 else self.source(step)
        ref = view(slot)
        return remote(ref, ref, self.sems.at[0, step, part], self.sems.at[1, step, part], "grid", self.mate)

    def relay(self, view, part, step):
        ref = view(self.source(step))
        return remote(ref, ref, self.sems.at[2, step, part], self.sems.at[3, step, part], "grid", self.mate)

    def relayed(self, view, part, step):
        ref = view(self.source_mate(step))
        return remote(ref, ref, self.sems.at[2, step, part], self.sems.at[3, step, part], "grid", self.mate)

    def start(self, view, part):
        for step in range(1, self.chips):
            self.own(view, part, step).start()
        self.own(view, part, 0).start()

    def forward(self, view, part):
        for step in range(1, self.chips):
            self.arrived(view, part, step).wait_recv()
            self.relay(view, part, step).start()

    def finish(self, view, part):
        self.arrived(view, part, 0).wait_recv()
        for step in range(1, self.chips):
            self.relayed(view, part, step).wait_recv()

    def drain(self, view, part):
        for step in range(self.chips):
            self.own(view, part, step).wait_send()
        for step in range(1, self.chips):
            self.relay(view, part, step).wait_send()


def gather_sems(size, parts):
    return pltpu.SemaphoreType.DMA((4, size // 2, parts))


def normalize(pieces, gains, shifts):
    width = pieces[0].shape[1] * len(pieces)
    total = sum(jnp.sum(piece, axis=1, keepdims=True) for piece in pieces)
    mean = total / width
    centred = [piece - mean for piece in pieces]
    square = sum(jnp.sum(piece * piece, axis=1, keepdims=True) for piece in centred)
    scale = lax.rsqrt(square / width + EPSILON)
    return [
        (piece * scale * gain + shift).astype(BF16)
        for piece, gain, shift in zip(centred, gains, shifts)
    ]


def project(pieces, weight_ref):
    width = pieces[0].shape[1]
    if width % LANES == 0:
        return jnp.dot(
            jnp.concatenate(pieces, axis=1), weight_ref[...], preferred_element_type=F32
        )
    total = None
    for index, piece in enumerate(pieces):
        term = jnp.dot(
            piece, weight_ref[index * width : (index + 1) * width, :], preferred_element_type=F32
        )
        total = term if total is None else total + term
    return total


def attend_kernel(
    size, count, parts, x_ref, *refs,
):
    vector_refs, refs = refs[:6], refs[6:]
    (
        wq_hbm, wk_hbm, wv_hbm, wo_ref,
        att_ref, xown_ref, affg_ref, wog_ref,
        xg_ref, wq_ref, wk_ref, wv_ref, q_ref, keys_ref, values_ref, qm_ref, max_ref, acc_ref,
        x_sems, aff_sems, right_sems, left_sems, wo_sems, load_sems,
    ) = refs
    rows, width = x_ref.shape
    heads = width // HEAD_DIM
    step_rows = rows // parts
    ctx = lax.axis_index("ctx")
    gather = GridGather(size, x_sems)
    small = GridGather(size, aff_sems)
    weights = GridGather(size, wo_sems)
    me = gather.me
    has_left = ctx > 0
    has_right = ctx < count - 1
    loads = [
        pltpu.make_async_copy(src, dst, load_sems.at[index])
        for index, (src, dst) in enumerate(
            ((wq_hbm, wq_ref), (wk_hbm, wk_ref), (wv_hbm, wv_ref), (wo_ref, wog_ref.at[me]))
        )
    ]
    for load in loads:
        load.start()
    barrier = pltpu.get_barrier_semaphore()
    greeted = gather.greet(barrier)

    @pl.when(has_left)
    def _():
        pl.semaphore_signal(barrier, inc=1, device_id={"ctx": ctx - 1}, device_id_type=MESH)

    @pl.when(has_right)
    def _():
        pl.semaphore_signal(barrier, inc=1, device_id={"ctx": ctx + 1}, device_id_type=MESH)

    xg_ref[ctx, me] = x_ref[...]
    for index, vector_ref in enumerate(vector_refs):
        affg_ref[me, index : index + 1, :] = vector_ref[...].astype(F32).reshape(1, width)
    affg_ref[me, 6:8, :] = jnp.zeros((2, width), F32)
    inner = (ctx + count - 1) // count + (2 * count - 2 - ctx) // count
    pl.semaphore_wait(barrier, greeted + inner)

    def block(slot, part):
        return lambda index: xg_ref.at[slot, index, pl.ds(part * step_rows, step_rows), :]

    def line(sems, slot, part, target):
        ref = block(slot, part)(me)
        return remote(ref, ref, sems.at[0, slot, part], sems.at[1, slot, part], "ctx", target)

    def place(order):
        short = jnp.minimum(ctx, count - 1 - ctx)
        near = (order + 1) // 2
        both = jnp.where(order % 2 == 1, ctx - near, ctx + near)
        rest = jnp.where(2 * ctx > count - 1, ctx - (order - short), ctx + (order - short))
        return jnp.where(order <= 2 * short, both, rest)

    def small_view(slot):
        return affg_ref.at[slot]

    def wo_view(slot):
        return wog_ref.at[slot]

    def advance(order):
        slot = place(order)
        for part in range(parts):

            @pl.when(slot < ctx)
            def _():
                line(right_sems, slot, part, ctx - 1).wait_recv()

                @pl.when(has_right)
                def _():
                    line(right_sems, slot, part, ctx + 1).start()

            @pl.when(slot > ctx)
            def _():
                line(left_sems, slot, part, ctx + 1).wait_recv()

                @pl.when(has_left)
                def _():
                    line(left_sems, slot, part, ctx - 1).start()

            gather.start(block(slot, part), slot * parts + part)

    def relay(order):
        slot = place(order)
        for part in range(parts):
            gather.forward(block(slot, part), slot * parts + part)

    small.start(small_view, 0)
    for part in range(parts):
        gather.start(block(ctx, part), ctx * parts + part)

        @pl.when(has_right)
        def _():
            line(right_sems, ctx, part, ctx + 1).start()

        @pl.when(has_left)
        def _():
            line(left_sems, ctx, part, ctx - 1).start()

    small.forward(small_view, 0)
    small.finish(small_view, 0)
    for load in loads:
        load.wait()
    scale = math.log2(math.e) / math.sqrt(HEAD_DIM)

    def prepare(slot, part):
        gather.finish(block(slot, part), slot * parts + part)
        span = slice(part * step_rows, (part + 1) * step_rows)
        gains = [affg_ref[index, 0:1, :] for index in range(size)]
        shifts = [affg_ref[index, 1:2, :] for index in range(size)]
        pieces = [xg_ref[slot, index, span, :].astype(F32) for index in range(size)]
        normed = normalize(pieces, gains, shifts)
        keys_ref[span, :] = project(normed, wk_ref).astype(BF16)
        values_ref[span, :] = project(normed, wv_ref).astype(BF16)
        return span, normed

    spans = []
    for head in range(heads):
        low = head * HEAD_DIM // LANES * LANES
        spans.append((low, min(low + LANES, width)))

    def attend(first):
        for head in range(heads):
            low, high = spans[head]
            keys = keys_ref[:, low:high]
            values = values_ref[:, low:high]
            extra = [jnp.ones((rows, LANES), BF16)]
            if high - low < LANES:
                extra = [jnp.zeros((rows, LANES - (high - low)), BF16)] + extra
            values = jnp.concatenate([values] + extra, axis=1)
            scores = lax.dot_general(
                qm_ref[head, :, 0 : high - low], keys, (((1,), (1,)), ((), ())),
                preferred_element_type=F32,
            )
            peak = jnp.max(scores, axis=1, keepdims=True)
            if first:
                peak = jnp.broadcast_to(peak, (rows, LANES))
            else:
                old = max_ref[head]
                peak = jnp.maximum(old, peak)
            soft = jnp.exp2(scores - jnp.concatenate([peak] * (rows // LANES), axis=1)).astype(BF16)
            mixed = jnp.dot(soft, values, preferred_element_type=F32)
            if first:
                acc_ref[head] = mixed
            else:
                factor = jnp.exp2(old - peak)
                acc_ref[head] = acc_ref[head] * jnp.concatenate([factor, factor], axis=1) + mixed
            max_ref[head] = peak

    relay(0)
    advance(1)
    for part in range(parts):
        span, normed = prepare(ctx, part)
        q_ref[span, :] = (project(normed, wq_ref) * scale).astype(BF16)
    keep = pltpu.make_async_copy(xg_ref.at[ctx], xown_ref, load_sems.at[4])
    keep.start()
    advance(2)
    relay(1)
    for head in range(heads):
        low, high = spans[head]
        pair = q_ref[:, low:high]
        lane = lax.broadcasted_iota(jnp.int32, pair.shape, 1)
        inside = lane // HEAD_DIM == (head * HEAD_DIM - low) // HEAD_DIM
        qm_ref[head, :, 0 : high - low] = jnp.where(inside, pair, jnp.zeros_like(pair))
    attend(True)

    @pl.loop(1, count)
    def _(order):
        slot = place(order)
        for part in range(parts):
            prepare(slot, part)

        @pl.when(order + 2 < count)
        def _():
            advance(order + 2)

        @pl.when(order == count - 3)
        def _():
            weights.start(wo_view, 0)

        @pl.when(order + 1 < count)
        def _():
            relay(order + 1)

        attend(False)

    for pair in range((heads + 1) // 2):
        low, high = spans[2 * pair]
        results = [
            acc_ref[head, :, 0:LANES] / acc_ref[head, :, LANES : 2 * LANES]
            for head in range(2 * pair, min(2 * pair + 2, heads))
        ]
        if len(results) == 2:
            lane = lax.broadcasted_iota(jnp.int32, (rows, LANES), 1)
            mixed = jnp.where(lane < HEAD_DIM, results[0], results[1])
        else:
            mixed = results[0]
        att_ref[:, low:high] = mixed[:, 0 : high - low].astype(BF16)

    weights.forward(wo_view, 0)
    weights.finish(wo_view, 0)
    weights.drain(wo_view, 0)
    small.drain(small_view, 0)
    keep.wait()

    @pl.loop(0, count)
    def _(slot):
        for part in range(parts):
            gather.drain(block(slot, part), slot * parts + part)

            @pl.when(has_right & (slot <= ctx))
            def _():
                line(right_sems, slot, part, ctx + 1).wait_send()

            @pl.when(has_left & (slot >= ctx))
            def _():
                line(left_sems, slot, part, ctx - 1).wait_send()


def last_kernel(
    size, count, parts, att_ref, xg_ref, affg_ref, wog_hbm, wgv_hbm, wgg_hbm, wp_hbm,
    taps_ref, out_ref,
    attg_ref, actg_ref, mid_ref, gated_ref, wo_ref, wgv_ref, wgg_ref, wp_ref,
    att_sems, act_sems, halo_sems, load_sems, wp_sems,
):
    rows, width = att_ref.shape
    step_rows = rows // parts
    ctx = lax.axis_index("ctx")
    attended = GridGather(size, att_sems)
    activated = GridGather(size, act_sems)
    me = attended.me
    has_left = ctx > 0
    has_right = ctx < count - 1

    def wp_block(index):
        if len(wp_hbm.shape) == 3:
            return wp_hbm.at[index]
        return wp_hbm.at[:, pl.ds(pl.multiple_of(index * width, LANES), width)]

    def wp_slot(index):
        return wp_ref.at[pl.ds(pl.multiple_of(index * width, HEAD_DIM), width), :]

    def send_wp(step):
        target = lax.rem(me + step, size)
        return remote(
            wp_block(target), wp_slot(me), wp_sems.at[0, step], wp_sems.at[1, step], "grid", target
        )

    def take_wp(step):
        source = lax.rem(me + size - step, size)
        return remote(
            wp_block(me), wp_slot(source), wp_sems.at[0, step], wp_sems.at[1, step], "grid", source
        )

    loads = [
        pltpu.make_async_copy(src, dst, load_sems.at[index])
        for index, (src, dst) in enumerate(
            ((wog_hbm, wo_ref), (wgv_hbm, wgv_ref), (wgg_hbm, wgg_ref), (wp_block(me), wp_slot(me)))
        )
    ]
    for load in loads:
        load.start()
    barrier = pltpu.get_barrier_semaphore()
    greeted = size - 1
    for step in range(1, size):
        pl.semaphore_signal(
            barrier, inc=1, device_id={"grid": lax.rem(me + step, size)}, device_id_type=MESH
        )

    @pl.when(has_left)
    def _():
        pl.semaphore_signal(barrier, inc=1, device_id={"ctx": ctx - 1}, device_id_type=MESH)

    @pl.when(has_right)
    def _():
        pl.semaphore_signal(barrier, inc=1, device_id={"ctx": ctx + 1}, device_id_type=MESH)

    attg_ref[me] = att_ref[...]
    inner = (ctx + count - 1) // count + (2 * count - 2 - ctx) // count
    pl.semaphore_wait(barrier, greeted + inner)

    def view(buffer, part):
        return lambda slot: buffer.at[slot, pl.ds(part * step_rows, step_rows), :]

    for part in range(parts):
        attended.start(view(attg_ref, part), part)
    for step in range(1, size):
        send_wp(step).start()

    @pl.when(jnp.logical_not(has_left))
    def _():
        gated_ref[0:PAD, :] = jnp.zeros((PAD, width), F32)

    @pl.when(jnp.logical_not(has_right))
    def _():
        gated_ref[PAD + rows : 2 * PAD + rows, :] = jnp.zeros((PAD, width), F32)

    def halo_left(index):
        return remote(
            gated_ref.at[PAD : 2 * PAD, :], gated_ref.at[PAD + rows : 2 * PAD + rows, :],
            halo_sems.at[0], halo_sems.at[1], "ctx", index,
        )

    def halo_right(index):
        return remote(
            gated_ref.at[rows : rows + PAD, :], gated_ref.at[0:PAD, :],
            halo_sems.at[2], halo_sems.at[3], "ctx", index,
        )

    attended.forward(view(attg_ref, 0), 0)
    for load in loads:
        load.wait()
    gains = [affg_ref[index, 2:3, :] for index in range(size)]
    shifts = [affg_ref[index, 3:4, :] for index in range(size)]
    for part in range(parts):
        if part + 1 < parts:
            attended.forward(view(attg_ref, part + 1), part + 1)
        attended.finish(view(attg_ref, part), part)
        span = slice(part * step_rows, (part + 1) * step_rows)
        products = project([attg_ref[index, span, :] for index in range(size)], wo_ref)
        pieces = []
        for column in range(size):
            total = products[:, column * width : (column + 1) * width]
            middle = (xg_ref[column, span, :].astype(F32) + total).astype(BF16)
            mid_ref[column, span, :] = middle
            pieces.append(middle.astype(F32))
        normed = normalize(pieces, gains, shifts)
        gate = project(normed, wgg_ref)
        value = project(normed, wgv_ref)
        gated = (value * (1.0 / (1.0 + jnp.exp(-gate)))).astype(BF16)
        gated_ref[PAD + part * step_rows : PAD + (part + 1) * step_rows, :] = gated.astype(F32)
        if part == 0:

            @pl.when(has_left)
            def _():
                halo_left(ctx - 1).start()

    @pl.when(has_right)
    def _():
        halo_right(ctx + 1).start()

    block_rows = min(32, step_rows)
    inner_parts = list(range(1, parts - 1))
    for order, part in enumerate(inner_parts + [0] + ([parts - 1] if parts > 1 else [])):
        if order == len(inner_parts):

            @pl.when(has_left)
            def _():
                halo_right(ctx - 1).wait_recv()

            @pl.when(has_right)
            def _():
                halo_left(ctx + 1).wait_recv()

        @pl.loop(0, step_rows // block_rows)
        def _(block):
            base = pl.multiple_of(part * step_rows + block * block_rows, block_rows)
            window = gated_ref[pl.ds(base, block_rows + 2 * PAD), :]
            total = jnp.zeros((block_rows, width), F32)
            for tap in range(KERNEL):
                low = tap + PAD - HALF
                total = total + taps_ref[tap : tap + 1, :] * window[low : low + block_rows, :]
            scaled = total * affg_ref[me, 4:5, :] + affg_ref[me, 5:6, :]
            result = scaled / (1.0 + jnp.exp(-scaled))
            actg_ref[me, pl.ds(base, block_rows), :] = result.astype(BF16)

        activated.start(view(actg_ref, part), part)

    sequence = inner_parts + [0] + ([parts - 1] if parts > 1 else [])
    activated.forward(view(actg_ref, sequence[0]), sequence[0])
    for step in range(1, size):
        take_wp(step).wait_recv()
    for order, part in enumerate(sequence):
        if order + 1 < parts:
            activated.forward(view(actg_ref, sequence[order + 1]), sequence[order + 1])
        activated.finish(view(actg_ref, part), part)
        span = slice(part * step_rows, (part + 1) * step_rows)
        total = mid_ref[me, span, :].astype(F32)
        total = total + project([actg_ref[index, span, :] for index in range(size)], wp_ref)
        out_ref[span, :] = total.astype(BF16)

    for part in range(parts):
        attended.drain(view(attg_ref, part), part)
        activated.drain(view(actg_ref, part), part)
    for step in range(1, size):
        send_wp(step).wait_send()

    @pl.when(has_left)
    def _():
        halo_left(ctx - 1).wait_send()

    @pl.when(has_right)
    def _():
        halo_right(ctx + 1).wait_send()


def params(number):
    return pltpu.CompilerParams(
        collective_id=number, has_side_effects=True, vmem_limit_bytes=VMEM_LIMIT
    )


def on_device(
    frames_in,
    norm1_gain,
    norm1_bias,
    w_query,
    w_key,
    w_value,
    w_out,
    norm2_gain,
    norm2_bias,
    w_glu_value,
    w_glu_gate,
    depth_kernel,
    bn_scale,
    bn_shift,
    w_proj,
):
    size = lax.axis_size("grid")
    count = lax.axis_size("ctx")
    rows, width = frames_in.shape
    full = width * size
    heads = width // HEAD_DIM
    vmem = pl.BlockSpec(memory_space=pltpu.VMEM)
    anywhere = pl.BlockSpec(memory_space=pl.ANY)
    dma = pltpu.SemaphoreType.DMA
    parts = 4

    def shape(dims, dtype=BF16):
        return jax.ShapeDtypeStruct(dims, dtype)

    wp_blocks = w_proj
    if width % LANES:
        wp_blocks = jnp.transpose(w_proj.reshape(width, size, width), (1, 0, 2))
    line_parts = 2
    weight = pltpu.VMEM((full, width), BF16)
    attended, frames_all, affine, wo_all = pl.pallas_call(
        lambda *refs: attend_kernel(size, count, line_parts, *refs),
        out_shape=(
            shape((rows, width)),
            shape((size, rows, width)),
            shape((size, 8, width), F32),
            shape((size, width, full)),
        ),
        in_specs=[vmem] * 7 + [anywhere] * 4,
        out_specs=(vmem, anywhere, vmem, anywhere),
        scratch_shapes=[
            pltpu.VMEM((count, size, rows, width), BF16),
            weight,
            weight,
            weight,
            pltpu.VMEM((rows, width), BF16),
            pltpu.VMEM((rows, width), BF16),
            pltpu.VMEM((rows, width), BF16),
            pltpu.VMEM((heads, rows, LANES), BF16),
            pltpu.VMEM((heads, rows, LANES), F32),
            pltpu.VMEM((heads, rows, 2 * LANES), F32),
            gather_sems(size, count * line_parts),
            gather_sems(size, 1),
            dma((2, count, line_parts)),
            dma((2, count, line_parts)),
            gather_sems(size, 1),
            dma((5,)),
        ],
        compiler_params=params(1),
        name="attend_ring",
    )(
        frames_in, norm1_gain, norm1_bias, norm2_gain, norm2_bias, bn_scale, bn_shift,
        w_query, w_key, w_value, w_out,
    )

    return pl.pallas_call(
        lambda *refs: last_kernel(size, count, parts, *refs),
        out_shape=shape((rows, width)),
        in_specs=[vmem, vmem, vmem] + [anywhere] * 4 + [vmem],
        out_specs=vmem,
        scratch_shapes=[
            pltpu.VMEM((size, rows, width), BF16),
            pltpu.VMEM((size, rows, width), BF16),
            pltpu.VMEM((size, rows, width), BF16),
            pltpu.VMEM((rows + 2 * PAD, width), F32),
            pltpu.VMEM((full, full), BF16),
            pltpu.VMEM((full, width), BF16),
            pltpu.VMEM((full, width), BF16),
            pltpu.VMEM((full, width), BF16),
            gather_sems(size, parts),
            gather_sems(size, parts),
            dma((4,)),
            dma((4,)),
            dma((2, size)),
        ],
        compiler_params=params(2),
        name="convolve_project",
    )(
        attended, frames_all, affine, wo_all.reshape(full, full), w_glu_value, w_glu_gate,
        wp_blocks, depth_kernel,
    )


def solution(mesh):
    return jax.shard_map(
        on_device,
        mesh=mesh,
        in_specs=(
            P(("parts", "ctx"), "grid"),
            P("grid"),
            P("grid"),
            P(None, "grid"),
            P(None, "grid"),
            P(None, "grid"),
            P("grid", None),
            P("grid"),
            P("grid"),
            P(None, "grid"),
            P(None, "grid"),
            P(None, "grid"),
            P("grid"),
            P("grid"),
            P("grid", None),
        ),
        out_specs=P(("parts", "ctx"), "grid"),
        check_vma=False,
    )
```

```python
import math

import jax
import jax.numpy as jnp
from jax import lax
from jax.experimental import pallas as pl
from jax.experimental.pallas import tpu as pltpu
from jax.sharding import PartitionSpec as P

HEAD_DIM = 64
KERNEL = 31
HALF = 15
EPSILON = 1e-05
LANES = 128
PAD = 16
MESH = pl.DeviceIdType.MESH
F32 = jnp.float32
BF16 = jnp.bfloat16
VMEM_LIMIT = 56 * 1024 * 1024


def remote(src, dst, send, recv, axis, index):
    return pltpu.make_async_remote_copy(
        src_ref=src,
        dst_ref=dst,
        send_sem=send,
        recv_sem=recv,
        device_id={axis: index},
        device_id_type=MESH,
    )


class GridGather:
    def __init__(self, size, sems):
        self.me = lax.axis_index("grid")
        self.chips = size // 2
        self.chip = self.me // 2
        self.core = self.me % 2
        self.mate = self.chip * 2 + 1 - self.core
        self.sems = sems

    def peer(self, step):
        return lax.rem(self.chip + step, self.chips) * 2 + self.core

    def source(self, step):
        return lax.rem(self.chip + self.chips - step, self.chips) * 2 + self.core

    def source_mate(self, step):
        return lax.rem(self.chip + self.chips - step, self.chips) * 2 + 1 - self.core

    def greet(self, barrier):
        pl.semaphore_signal(barrier, inc=1, device_id={"grid": self.mate}, device_id_type=MESH)
        for step in range(1, self.chips):
            pl.semaphore_signal(
                barrier, inc=1, device_id={"grid": self.peer(step)}, device_id_type=MESH
            )
        return self.chips

    def own(self, view, part, step):
        ref = view(self.me)
        target = self.mate if step == 0 else self.peer(step)
        return remote(ref, ref, self.sems.at[0, step, part], self.sems.at[1, step, part], "grid", target)

    def arrived(self, view, part, step):
        slot = self.mate if step == 0 else self.source(step)
        ref = view(slot)
        return remote(ref, ref, self.sems.at[0, step, part], self.sems.at[1, step, part], "grid", self.mate)

    def relay(self, view, part, step):
        ref = view(self.source(step))
        return remote(ref, ref, self.sems.at[2, step, part], self.sems.at[3, step, part], "grid", self.mate)

    def relayed(self, view, part, step):
        ref = view(self.source_mate(step))
        return remote(ref, ref, self.sems.at[2, step, part], self.sems.at[3, step, part], "grid", self.mate)

    def start(self, view, part):
        for step in range(1, self.chips):
            self.own(view, part, step).start()
        self.own(view, part, 0).start()

    def forward(self, view, part):
        for step in range(1, self.chips):
            self.arrived(view, part, step).wait_recv()
            self.relay(view, part, step).start()

    def finish(self, view, part):
        self.arrived(view, part, 0).wait_recv()
        for step in range(1, self.chips):
            self.relayed(view, part, step).wait_recv()

    def drain(self, view, part):
        for step in range(self.chips):
            self.own(view, part, step).wait_send()
        for step in range(1, self.chips):
            self.relay(view, part, step).wait_send()


def gather_sems(size, parts):
    return pltpu.SemaphoreType.DMA((4, size // 2, parts))


def normalize(pieces, gains, shifts):
    width = pieces[0].shape[1] * len(pieces)
    total = sum(jnp.sum(piece, axis=1, keepdims=True) for piece in pieces)
    mean = total / width
    centred = [piece - mean for piece in pieces]
    square = sum(jnp.sum(piece * piece, axis=1, keepdims=True) for piece in centred)
    scale = lax.rsqrt(square / width + EPSILON)
    return [
        (piece * scale * gain + shift).astype(BF16)
        for piece, gain, shift in zip(centred, gains, shifts)
    ]


def project(pieces, weight_ref):
    width = pieces[0].shape[1]
    if width % LANES == 0:
        return jnp.dot(
            jnp.concatenate(pieces, axis=1), weight_ref[...], preferred_element_type=F32
        )
    total = None
    for index, piece in enumerate(pieces):
        term = jnp.dot(
            piece, weight_ref[index * width : (index + 1) * width, :], preferred_element_type=F32
        )
        total = term if total is None else total + term
    return total


def attend_kernel(
    size, count, parts, x_ref, *refs,
):
    vector_refs, refs = refs[:6], refs[6:]
    (
        wq_hbm, wk_hbm, wv_hbm, wo_ref, wp_ref,
        att_ref, xg_ref, affg_ref, wog_ref, wpg_ref,
        wq_ref, wk_ref, wv_ref, q_ref, kvg_ref, qm_ref, max_ref, acc_ref,
        x_sems, aff_sems, right_sems, left_sems, wo_sems, wp_sems, load_sems, matrix_sems,
    ) = refs
    rows, width = x_ref.shape
    heads = width // HEAD_DIM
    step_rows = rows // parts
    ctx = lax.axis_index("ctx")
    gather = GridGather(size, wo_sems)
    frames = GridGather(size, x_sems)
    small = GridGather(size, aff_sems)
    me = gather.me
    has_left = ctx > 0
    has_right = ctx < count - 1
    matrices = [
        pltpu.make_async_copy(src, dst, matrix_sems.at[index])
        for index, (src, dst) in enumerate(((wq_hbm, wq_ref), (wk_hbm, wk_ref), (wv_hbm, wv_ref)))
    ]
    for load in matrices:
        load.start()
    barrier = pltpu.get_barrier_semaphore()
    for step in range(1, size):
        pl.semaphore_signal(
            barrier, inc=1, device_id={"grid": lax.rem(me + step, size)}, device_id_type=MESH
        )

    @pl.when(has_left)
    def _():
        pl.semaphore_signal(barrier, inc=1, device_id={"ctx": ctx - 1}, device_id_type=MESH)

    @pl.when(has_right)
    def _():
        pl.semaphore_signal(barrier, inc=1, device_id={"ctx": ctx + 1}, device_id_type=MESH)

    xg_ref[me] = x_ref[...]
    for index, vector_ref in enumerate(vector_refs):
        affg_ref[me, index : index + 1, :] = vector_ref[...].astype(F32).reshape(1, width)
    affg_ref[me, 6:8, :] = jnp.zeros((2, width), F32)
    inner = (ctx + count - 1) // count + (2 * count - 2 - ctx) // count
    pl.semaphore_wait(barrier, size - 1 + inner)

    def block(slot, part):
        return kvg_ref.at[slot, :, pl.ds(part * step_rows, step_rows), :]

    def to_right(step, part):
        ref = block(ctx - step, part)
        return remote(ref, ref, right_sems.at[0, step, part], right_sems.at[1, step, part], "ctx", ctx + 1)

    def from_left(step, part):
        ref = block(ctx - 1 - step, part)
        return remote(ref, ref, right_sems.at[0, step, part], right_sems.at[1, step, part], "ctx", ctx - 1)

    def to_left(step, part):
        ref = block(ctx + step, part)
        return remote(ref, ref, left_sems.at[0, step, part], left_sems.at[1, step, part], "ctx", ctx - 1)

    def from_right(step, part):
        ref = block(ctx + 1 + step, part)
        return remote(ref, ref, left_sems.at[0, step, part], left_sems.at[1, step, part], "ctx", ctx + 1)

    def frames_view(part):
        return lambda slot: xg_ref.at[slot, pl.ds(part * step_rows, step_rows), :]

    def small_view(slot):
        return affg_ref.at[slot]

    small.start(small_view, 0)
    for part in range(parts):
        frames.start(frames_view(part), part)
    small.forward(small_view, 0)
    frames.forward(frames_view(0), 0)
    small.finish(small_view, 0)
    for load in matrices:
        load.wait()
    gains = [affg_ref[index, 0:1, :] for index in range(size)]
    shifts = [affg_ref[index, 1:2, :] for index in range(size)]
    scale = math.log2(math.e) / math.sqrt(HEAD_DIM)
    for part in range(parts):
        if part + 1 < parts:
            frames.forward(frames_view(part + 1), part + 1)
        frames.finish(frames_view(part), part)
        span = slice(part * step_rows, (part + 1) * step_rows)
        normed = normalize(
            [xg_ref[index, span, :].astype(F32) for index in range(size)], gains, shifts
        )
        kvg_ref[ctx, 0, span, :] = project(normed, wk_ref).astype(BF16)
        kvg_ref[ctx, 1, span, :] = project(normed, wv_ref).astype(BF16)

        @pl.when(has_right)
        def _():
            to_right(0, part).start()

        @pl.when(has_left)
        def _():
            to_left(0, part).start()

        q_ref[span, :] = (project(normed, wq_ref) * scale).astype(BF16)

    def wo_view(slot):
        return wog_ref.at[slot]

    for step in range(gather.chips):
        target = gather.mate if step == 0 else gather.peer(step)
        remote(wo_ref, wog_ref.at[me], wo_sems.at[0, step, 0], wo_sems.at[1, step, 0], "grid", target).start()

    def wp_block(index):
        if len(wp_ref.shape) == 3:
            return wp_ref.at[index]
        return wp_ref.at[:, pl.ds(pl.multiple_of(index * width, LANES), width)]

    def send_wp(step):
        target = lax.rem(me + step, size)
        return remote(wp_block(target), wpg_ref.at[me], wp_sems.at[0, step], wp_sems.at[1, step], "grid", target)

    for step in range(1, size):
        send_wp(step).start()
    loads = [
        pltpu.make_async_copy(wo_ref, wog_ref.at[me], load_sems.at[0]),
        pltpu.make_async_copy(wp_block(me), wpg_ref.at[me], load_sems.at[1]),
    ]
    for load in loads:
        load.start()

    spans = []
    for head in range(heads):
        low = head * HEAD_DIM // LANES * LANES
        high = min(low + LANES, width)
        spans.append((low, high))
        pair = q_ref[:, low:high]
        lane = lax.broadcasted_iota(jnp.int32, pair.shape, 1)
        inside = lane // HEAD_DIM == (head * HEAD_DIM - low) // HEAD_DIM
        qm_ref[head, :, 0 : high - low] = jnp.where(inside, pair, jnp.zeros_like(pair))

    def attend(slot, first):
        for head in range(heads):
            low, high = spans[head]
            keys = kvg_ref[slot, 0, :, low:high]
            values = kvg_ref[slot, 1, :, low:high]
            extra = [jnp.ones((rows, LANES), BF16)]
            if high - low < LANES:
                extra = [jnp.zeros((rows, LANES - (high - low)), BF16)] + extra
            values = jnp.concatenate([values] + extra, axis=1)
            scores = lax.dot_general(
                qm_ref[head, :, 0 : high - low], keys, (((1,), (1,)), ((), ())),
                preferred_element_type=F32,
            )
            peak = jnp.max(scores, axis=1, keepdims=True)
            if first:
                peak = jnp.broadcast_to(peak, (rows, LANES))
                soft = jnp.exp2(scores - jnp.concatenate([peak] * (rows // LANES), axis=1)).astype(BF16)
                acc_ref[head] = jnp.dot(soft, values, preferred_element_type=F32)
            else:
                old = max_ref[head]
                peak = jnp.maximum(old, peak)
                factor = jnp.exp2(old - peak)
                soft = jnp.exp2(scores - jnp.concatenate([peak] * (rows // LANES), axis=1)).astype(BF16)
                acc_ref[head] = acc_ref[head] * jnp.concatenate([factor, factor], axis=1) + jnp.dot(
                    soft, values, preferred_element_type=F32
                )
            max_ref[head] = peak

    attend(ctx, True)

    @pl.loop(0, count - 1)
    def _(step):
        left_there = ctx - 1 - step >= 0
        right_there = ctx + 1 + step <= count - 1
        for part in range(parts):

            @pl.when(left_there)
            def _():
                from_left(step, part).wait_recv()

                @pl.when(has_right)
                def _():
                    to_right(step + 1, part).start()

            @pl.when(right_there)
            def _():
                from_right(step, part).wait_recv()

                @pl.when(has_left)
                def _():
                    to_left(step + 1, part).start()

        @pl.when(step == count - 2)
        def _():
            gather.forward(wo_view, 0)

        @pl.loop(0, 2)
        def _(side):
            slot = jnp.where(side == 0, ctx - 1 - step, ctx + 1 + step)

            @pl.when((slot >= 0) & (slot <= count - 1))
            def _():
                attend(slot, False)

    for pair in range((heads + 1) // 2):
        low, high = spans[2 * pair]
        results = [
            acc_ref[head, :, 0:LANES] / acc_ref[head, :, LANES : 2 * LANES]
            for head in range(2 * pair, min(2 * pair + 2, heads))
        ]
        if len(results) == 2:
            lane = lax.broadcasted_iota(jnp.int32, (rows, LANES), 1)
            mixed = jnp.where(lane < HEAD_DIM, results[0], results[1])
        else:
            mixed = results[0]
        att_ref[:, low:high] = mixed[:, 0 : high - low].astype(BF16)

    small.drain(small_view, 0)
    for part in range(parts):
        frames.drain(frames_view(part), part)
    gather.finish(wo_view, 0)
    for step in range(gather.chips):
        target = gather.mate if step == 0 else gather.peer(step)
        remote(wo_ref, wog_ref.at[me], wo_sems.at[0, step, 0], wo_sems.at[1, step, 0], "grid", target).wait_send()
    for step in range(1, gather.chips):
        gather.relay(wo_view, 0, step).wait_send()
    for step in range(1, size):
        send_wp(step).wait_send()
        source = lax.rem(me + size - step, size)
        remote(wp_block(me), wpg_ref.at[source], wp_sems.at[0, step], wp_sems.at[1, step], "grid", source).wait_recv()
    for load in loads:
        load.wait()

    @pl.loop(0, count - 1)
    def _(step):
        for part in range(parts):

            @pl.when(has_right & (ctx - step >= 0))
            def _():
                to_right(step, part).wait_send()

            @pl.when(has_left & (ctx + step <= count - 1))
            def _():
                to_left(step, part).wait_send()


def last_kernel(
    size, count, parts, att_ref, xg_ref, affg_ref, wog_hbm, wgv_hbm, wgg_hbm, wpg_hbm,
    taps_ref, out_ref,
    attg_ref, actg_ref, mid_ref, gated_ref, wo_ref, wgv_ref, wgg_ref, wp_ref,
    att_sems, act_sems, halo_sems, load_sems,
):
    rows, width = att_ref.shape
    step_rows = rows // parts
    ctx = lax.axis_index("ctx")
    attended = GridGather(size, att_sems)
    activated = GridGather(size, act_sems)
    me = attended.me
    has_left = ctx > 0
    has_right = ctx < count - 1
    loads = [
        pltpu.make_async_copy(src, dst, load_sems.at[index])
        for index, (src, dst) in enumerate(
            ((wog_hbm, wo_ref), (wgv_hbm, wgv_ref), (wgg_hbm, wgg_ref), (wpg_hbm, wp_ref))
        )
    ]
    for load in loads:
        load.start()
    barrier = pltpu.get_barrier_semaphore()
    greeted = attended.greet(barrier)

    @pl.when(has_left)
    def _():
        pl.semaphore_signal(barrier, inc=1, device_id={"ctx": ctx - 1}, device_id_type=MESH)

    @pl.when(has_right)
    def _():
        pl.semaphore_signal(barrier, inc=1, device_id={"ctx": ctx + 1}, device_id_type=MESH)

    attg_ref[me] = att_ref[...]
    inner = (ctx + count - 1) // count + (2 * count - 2 - ctx) // count
    pl.semaphore_wait(barrier, greeted + inner)

    def view(buffer, part):
        return lambda slot: buffer.at[slot, pl.ds(part * step_rows, step_rows), :]

    for part in range(parts):
        attended.start(view(attg_ref, part), part)

    @pl.when(jnp.logical_not(has_left))
    def _():
        gated_ref[0:PAD, :] = jnp.zeros((PAD, width), F32)

    @pl.when(jnp.logical_not(has_right))
    def _():
        gated_ref[PAD + rows : 2 * PAD + rows, :] = jnp.zeros((PAD, width), F32)

    def halo_left(index):
        return remote(
            gated_ref.at[PAD : 2 * PAD, :], gated_ref.at[PAD + rows : 2 * PAD + rows, :],
            halo_sems.at[0], halo_sems.at[1], "ctx", index,
        )

    def halo_right(index):
        return remote(
            gated_ref.at[rows : rows + PAD, :], gated_ref.at[0:PAD, :],
            halo_sems.at[2], halo_sems.at[3], "ctx", index,
        )

    attended.forward(view(attg_ref, 0), 0)
    for load in loads:
        load.wait()
    gains = [affg_ref[index, 2:3, :] for index in range(size)]
    shifts = [affg_ref[index, 3:4, :] for index in range(size)]
    for part in range(parts):
        if part + 1 < parts:
            attended.forward(view(attg_ref, part + 1), part + 1)
        attended.finish(view(attg_ref, part), part)
        span = slice(part * step_rows, (part + 1) * step_rows)
        sources = [attg_ref[index, span, :] for index in range(size)]
        products = project(sources, wo_ref)
        pieces = []
        for column in range(size):
            total = products[:, column * width : (column + 1) * width]
            middle = (xg_ref[column, span, :].astype(F32) + total).astype(BF16)
            mid_ref[column, span, :] = middle
            pieces.append(middle.astype(F32))
        normed = normalize(pieces, gains, shifts)
        gate = project(normed, wgg_ref)
        value = project(normed, wgv_ref)
        gated = (value * (1.0 / (1.0 + jnp.exp(-gate)))).astype(BF16)
        gated_ref[PAD + part * step_rows : PAD + (part + 1) * step_rows, :] = gated.astype(F32)
        if part == 0:

            @pl.when(has_left)
            def _():
                halo_left(ctx - 1).start()

    @pl.when(has_right)
    def _():
        halo_right(ctx + 1).start()

    block_rows = min(32, step_rows)
    inner_parts = list(range(1, parts - 1))
    for order, part in enumerate(inner_parts + [0] + ([parts - 1] if parts > 1 else [])):
        if order == len(inner_parts):

            @pl.when(has_left)
            def _():
                halo_right(ctx - 1).wait_recv()

            @pl.when(has_right)
            def _():
                halo_left(ctx + 1).wait_recv()

        @pl.loop(0, step_rows // block_rows)
        def _(block):
            base = pl.multiple_of(part * step_rows + block * block_rows, block_rows)
            window = gated_ref[pl.ds(base, block_rows + 2 * PAD), :]
            total = jnp.zeros((block_rows, width), F32)
            for tap in range(KERNEL):
                low = tap + PAD - HALF
                total = total + taps_ref[tap : tap + 1, :] * window[low : low + block_rows, :]
            scaled = total * affg_ref[me, 4:5, :] + affg_ref[me, 5:6, :]
            result = scaled / (1.0 + jnp.exp(-scaled))
            actg_ref[me, pl.ds(base, block_rows), :] = result.astype(BF16)

        activated.start(view(actg_ref, part), part)

    sequence = inner_parts + [0] + ([parts - 1] if parts > 1 else [])
    activated.forward(view(actg_ref, sequence[0]), sequence[0])
    for order, part in enumerate(sequence):
        if order + 1 < parts:
            activated.forward(view(actg_ref, sequence[order + 1]), sequence[order + 1])
        activated.finish(view(actg_ref, part), part)
        span = slice(part * step_rows, (part + 1) * step_rows)
        total = mid_ref[me, span, :].astype(F32)
        total = total + project([actg_ref[index, span, :] for index in range(size)], wp_ref)
        out_ref[span, :] = total.astype(BF16)

    for part in range(parts):
        attended.drain(view(attg_ref, part), part)
        activated.drain(view(actg_ref, part), part)

    @pl.when(has_left)
    def _():
        halo_left(ctx - 1).wait_send()

    @pl.when(has_right)
    def _():
        halo_right(ctx + 1).wait_send()


def params(number):
    return pltpu.CompilerParams(
        collective_id=number, has_side_effects=True, vmem_limit_bytes=VMEM_LIMIT
    )


def on_device(
    frames_in,
    norm1_gain,
    norm1_bias,
    w_query,
    w_key,
    w_value,
    w_out,
    norm2_gain,
    norm2_bias,
    w_glu_value,
    w_glu_gate,
    depth_kernel,
    bn_scale,
    bn_shift,
    w_proj,
):
    size = lax.axis_size("grid")
    count = lax.axis_size("ctx")
    rows, width = frames_in.shape
    full = width * size
    heads = width // HEAD_DIM
    vmem = pl.BlockSpec(memory_space=pltpu.VMEM)
    anywhere = pl.BlockSpec(memory_space=pl.ANY)
    dma = pltpu.SemaphoreType.DMA
    parts = 4

    def shape(dims, dtype=BF16):
        return jax.ShapeDtypeStruct(dims, dtype)

    wp_blocks = w_proj
    if width % LANES:
        wp_blocks = jnp.transpose(w_proj.reshape(width, size, width), (1, 0, 2))
    weight = pltpu.VMEM((full, width), BF16)
    attended, xg, affg, wo_all, wp_all = pl.pallas_call(
        lambda *refs: attend_kernel(size, count, parts, *refs),
        out_shape=(
            shape((rows, width)),
            shape((size, rows, width)),
            shape((size, 8, width), F32),
            shape((size, width, full)),
            shape((size, width, width)),
        ),
        in_specs=[vmem] * 7 + [anywhere] * 5,
        out_specs=(vmem, vmem, vmem, anywhere, anywhere),
        scratch_shapes=[
            weight,
            weight,
            weight,
            pltpu.VMEM((rows, width), BF16),
            pltpu.VMEM((count, 2, rows, width), BF16),
            pltpu.VMEM((heads, rows, LANES), BF16),
            pltpu.VMEM((heads, rows, LANES), F32),
            pltpu.VMEM((heads, rows, 2 * LANES), F32),
            gather_sems(size, parts),
            gather_sems(size, 1),
            dma((2, count, parts)),
            dma((2, count, parts)),
            gather_sems(size, 1),
            dma((2, size)),
            dma((2,)),
            dma((3,)),
        ],
        compiler_params=params(1),
        name="attend_ring",
    )(
        frames_in, norm1_gain, norm1_bias, norm2_gain, norm2_bias, bn_scale, bn_shift,
        w_query, w_key, w_value, w_out, wp_blocks,
    )

    return pl.pallas_call(
        lambda *refs: last_kernel(size, count, parts, *refs),
        out_shape=shape((rows, width)),
        in_specs=[vmem, vmem, vmem] + [anywhere] * 4 + [vmem],
        out_specs=vmem,
        scratch_shapes=[
            pltpu.VMEM((size, rows, width), BF16),
            pltpu.VMEM((size, rows, width), BF16),
            pltpu.VMEM((size, rows, width), BF16),
            pltpu.VMEM((rows + 2 * PAD, width), F32),
            pltpu.VMEM((full, full), BF16),
            pltpu.VMEM((full, width), BF16),
            pltpu.VMEM((full, width), BF16),
            pltpu.VMEM((full, width), BF16),
            gather_sems(size, parts),
            gather_sems(size, parts),
            dma((4,)),
            dma((4,)),
        ],
        compiler_params=params(2),
        name="convolve_project",
    )(
        attended, xg, affg, wo_all.reshape(full, full), w_glu_value, w_glu_gate,
        wp_all.reshape(full, width), depth_kernel,
    )


def solution(mesh):
    return jax.shard_map(
        on_device,
        mesh=mesh,
        in_specs=(
            P(("parts", "ctx"), "grid"),
            P("grid"),
            P("grid"),
            P(None, "grid"),
            P(None, "grid"),
            P(None, "grid"),
            P("grid", None),
            P("grid"),
            P("grid"),
            P(None, "grid"),
            P(None, "grid"),
            P(None, "grid"),
            P("grid"),
            P("grid"),
            P("grid", None),
        ),
        out_specs=P(("parts", "ctx"), "grid"),
        check_vma=False,
    )
```

```python
import math

import jax
import jax.numpy as jnp
from jax import lax
from jax.experimental import pallas as pl
from jax.experimental.pallas import tpu as pltpu
from jax.sharding import PartitionSpec as P

HEAD_DIM = 64
KERNEL = 31
HALF = 15
EPSILON = 1e-05
LANES = 128
PAD = 16
MESH = pl.DeviceIdType.MESH
F32 = jnp.float32
BF16 = jnp.bfloat16
VMEM_LIMIT = 56 * 1024 * 1024


def remote(src, dst, send, recv, axis, index):
    return pltpu.make_async_remote_copy(
        src_ref=src,
        dst_ref=dst,
        send_sem=send,
        recv_sem=recv,
        device_id={axis: index},
        device_id_type=MESH,
    )


class GridGather:
    def __init__(self, size, sems):
        self.me = lax.axis_index("grid")
        self.chips = size // 2
        self.chip = self.me // 2
        self.core = self.me % 2
        self.mate = self.chip * 2 + 1 - self.core
        self.sems = sems

    def peer(self, step):
        return lax.rem(self.chip + step, self.chips) * 2 + self.core

    def source(self, step):
        return lax.rem(self.chip + self.chips - step, self.chips) * 2 + self.core

    def source_mate(self, step):
        return lax.rem(self.chip + self.chips - step, self.chips) * 2 + 1 - self.core

    def greet(self, barrier):
        pl.semaphore_signal(barrier, inc=1, device_id={"grid": self.mate}, device_id_type=MESH)
        for step in range(1, self.chips):
            pl.semaphore_signal(
                barrier, inc=1, device_id={"grid": self.peer(step)}, device_id_type=MESH
            )
        return self.chips

    def own(self, view, part, step):
        ref = view(self.me)
        target = self.mate if step == 0 else self.peer(step)
        return remote(ref, ref, self.sems.at[0, step, part], self.sems.at[1, step, part], "grid", target)

    def arrived(self, view, part, step):
        slot = self.mate if step == 0 else self.source(step)
        ref = view(slot)
        return remote(ref, ref, self.sems.at[0, step, part], self.sems.at[1, step, part], "grid", self.mate)

    def relay(self, view, part, step):
        ref = view(self.source(step))
        return remote(ref, ref, self.sems.at[2, step, part], self.sems.at[3, step, part], "grid", self.mate)

    def relayed(self, view, part, step):
        ref = view(self.source_mate(step))
        return remote(ref, ref, self.sems.at[2, step, part], self.sems.at[3, step, part], "grid", self.mate)

    def start(self, view, part):
        for step in range(1, self.chips):
            self.own(view, part, step).start()
        self.own(view, part, 0).start()

    def forward(self, view, part):
        for step in range(1, self.chips):
            self.arrived(view, part, step).wait_recv()
            self.relay(view, part, step).start()

    def finish(self, view, part):
        self.arrived(view, part, 0).wait_recv()
        for step in range(1, self.chips):
            self.relayed(view, part, step).wait_recv()

    def drain(self, view, part):
        for step in range(self.chips):
            self.own(view, part, step).wait_send()
        for step in range(1, self.chips):
            self.relay(view, part, step).wait_send()


def gather_sems(size, parts):
    return pltpu.SemaphoreType.DMA((4, size // 2, parts))


def normalize(pieces, gains, shifts):
    width = pieces[0].shape[1] * len(pieces)
    total = sum(jnp.sum(piece, axis=1, keepdims=True) for piece in pieces)
    mean = total / width
    centred = [piece - mean for piece in pieces]
    square = sum(jnp.sum(piece * piece, axis=1, keepdims=True) for piece in centred)
    scale = lax.rsqrt(square / width + EPSILON)
    return [
        (piece * scale * gain + shift).astype(BF16)
        for piece, gain, shift in zip(centred, gains, shifts)
    ]


def project(pieces, weight_ref):
    width = pieces[0].shape[1]
    if width % LANES == 0:
        return jnp.dot(
            jnp.concatenate(pieces, axis=1), weight_ref[...], preferred_element_type=F32
        )
    total = None
    for index, piece in enumerate(pieces):
        term = jnp.dot(
            piece, weight_ref[index * width : (index + 1) * width, :], preferred_element_type=F32
        )
        total = term if total is None else total + term
    return total


def attend_kernel(
    size, count, parts, x_ref, *refs,
):
    vector_refs, refs = refs[:6], refs[6:]
    (
        wq_hbm, wk_hbm, wv_hbm, wo_ref,
        att_ref, xg_ref, affg_ref, wog_ref,
        wq_ref, wk_ref, wv_ref, q_ref, kvg_ref, qm_ref, max_ref, acc_ref,
        x_sems, aff_sems, right_sems, left_sems, wo_sems, load_sems, matrix_sems,
    ) = refs
    rows, width = x_ref.shape
    heads = width // HEAD_DIM
    step_rows = rows // parts
    ctx = lax.axis_index("ctx")
    gather = GridGather(size, wo_sems)
    frames = GridGather(size, x_sems)
    small = GridGather(size, aff_sems)
    me = gather.me
    has_left = ctx > 0
    has_right = ctx < count - 1
    matrices = [
        pltpu.make_async_copy(src, dst, matrix_sems.at[index])
        for index, (src, dst) in enumerate(((wq_hbm, wq_ref), (wk_hbm, wk_ref), (wv_hbm, wv_ref)))
    ]
    for load in matrices:
        load.start()
    barrier = pltpu.get_barrier_semaphore()
    for step in range(1, size):
        pl.semaphore_signal(
            barrier, inc=1, device_id={"grid": lax.rem(me + step, size)}, device_id_type=MESH
        )

    @pl.when(has_left)
    def _():
        pl.semaphore_signal(barrier, inc=1, device_id={"ctx": ctx - 1}, device_id_type=MESH)

    @pl.when(has_right)
    def _():
        pl.semaphore_signal(barrier, inc=1, device_id={"ctx": ctx + 1}, device_id_type=MESH)

    xg_ref[me] = x_ref[...]
    for index, vector_ref in enumerate(vector_refs):
        affg_ref[me, index : index + 1, :] = vector_ref[...].astype(F32).reshape(1, width)
    affg_ref[me, 6:8, :] = jnp.zeros((2, width), F32)
    inner = (ctx + count - 1) // count + (2 * count - 2 - ctx) // count
    pl.semaphore_wait(barrier, size - 1 + inner)

    def block(slot, part):
        return kvg_ref.at[slot, :, pl.ds(part * step_rows, step_rows), :]

    def to_right(step, part):
        ref = block(ctx - step, part)
        return remote(ref, ref, right_sems.at[0, step, part], right_sems.at[1, step, part], "ctx", ctx + 1)

    def from_left(step, part):
        ref = block(ctx - 1 - step, part)
        return remote(ref, ref, right_sems.at[0, step, part], right_sems.at[1, step, part], "ctx", ctx - 1)

    def to_left(step, part):
        ref = block(ctx + step, part)
        return remote(ref, ref, left_sems.at[0, step, part], left_sems.at[1, step, part], "ctx", ctx - 1)

    def from_right(step, part):
        ref = block(ctx + 1 + step, part)
        return remote(ref, ref, left_sems.at[0, step, part], left_sems.at[1, step, part], "ctx", ctx + 1)

    def frames_view(part):
        return lambda slot: xg_ref.at[slot, pl.ds(part * step_rows, step_rows), :]

    def small_view(slot):
        return affg_ref.at[slot]

    small.start(small_view, 0)
    for part in range(parts):
        frames.start(frames_view(part), part)
    small.forward(small_view, 0)
    frames.forward(frames_view(0), 0)
    small.finish(small_view, 0)
    for load in matrices:
        load.wait()
    gains = [affg_ref[index, 0:1, :] for index in range(size)]
    shifts = [affg_ref[index, 1:2, :] for index in range(size)]
    scale = math.log2(math.e) / math.sqrt(HEAD_DIM)
    for part in range(parts):
        if part + 1 < parts:
            frames.forward(frames_view(part + 1), part + 1)
        frames.finish(frames_view(part), part)
        span = slice(part * step_rows, (part + 1) * step_rows)
        normed = normalize(
            [xg_ref[index, span, :].astype(F32) for index in range(size)], gains, shifts
        )
        kvg_ref[ctx, 0, span, :] = project(normed, wk_ref).astype(BF16)
        kvg_ref[ctx, 1, span, :] = project(normed, wv_ref).astype(BF16)

        @pl.when(has_right)
        def _():
            to_right(0, part).start()

        @pl.when(has_left)
        def _():
            to_left(0, part).start()

        q_ref[span, :] = (project(normed, wq_ref) * scale).astype(BF16)

    def wo_view(slot):
        return wog_ref.at[slot]

    for step in range(gather.chips):
        target = gather.mate if step == 0 else gather.peer(step)
        remote(wo_ref, wog_ref.at[me], wo_sems.at[0, step, 0], wo_sems.at[1, step, 0], "grid", target).start()

    loads = [
        pltpu.make_async_copy(wo_ref, wog_ref.at[me], load_sems.at[0]),
    ]
    for load in loads:
        load.start()

    spans = []
    for head in range(heads):
        low = head * HEAD_DIM // LANES * LANES
        high = min(low + LANES, width)
        spans.append((low, high))
        pair = q_ref[:, low:high]
        lane = lax.broadcasted_iota(jnp.int32, pair.shape, 1)
        inside = lane // HEAD_DIM == (head * HEAD_DIM - low) // HEAD_DIM
        qm_ref[head, :, 0 : high - low] = jnp.where(inside, pair, jnp.zeros_like(pair))

    def attend(slot, first):
        for head in range(heads):
            low, high = spans[head]
            keys = kvg_ref[slot, 0, :, low:high]
            values = kvg_ref[slot, 1, :, low:high]
            extra = [jnp.ones((rows, LANES), BF16)]
            if high - low < LANES:
                extra = [jnp.zeros((rows, LANES - (high - low)), BF16)] + extra
            values = jnp.concatenate([values] + extra, axis=1)
            scores = lax.dot_general(
                qm_ref[head, :, 0 : high - low], keys, (((1,), (1,)), ((), ())),
                preferred_element_type=F32,
            )
            peak = jnp.max(scores, axis=1, keepdims=True)
            if first:
                peak = jnp.broadcast_to(peak, (rows, LANES))
                soft = jnp.exp2(scores - jnp.concatenate([peak] * (rows // LANES), axis=1)).astype(BF16)
                acc_ref[head] = jnp.dot(soft, values, preferred_element_type=F32)
            else:
                old = max_ref[head]
                peak = jnp.maximum(old, peak)
                factor = jnp.exp2(old - peak)
                soft = jnp.exp2(scores - jnp.concatenate([peak] * (rows // LANES), axis=1)).astype(BF16)
                acc_ref[head] = acc_ref[head] * jnp.concatenate([factor, factor], axis=1) + jnp.dot(
                    soft, values, preferred_element_type=F32
                )
            max_ref[head] = peak

    attend(ctx, True)

    @pl.loop(0, count - 1)
    def _(step):
        left_there = ctx - 1 - step >= 0
        right_there = ctx + 1 + step <= count - 1
        for part in range(parts):

            @pl.when(left_there)
            def _():
                from_left(step, part).wait_recv()

                @pl.when(has_right)
                def _():
                    to_right(step + 1, part).start()

            @pl.when(right_there)
            def _():
                from_right(step, part).wait_recv()

                @pl.when(has_left)
                def _():
                    to_left(step + 1, part).start()

        @pl.when(step == count - 2)
        def _():
            gather.forward(wo_view, 0)

        @pl.loop(0, 2)
        def _(side):
            slot = jnp.where(side == 0, ctx - 1 - step, ctx + 1 + step)

            @pl.when((slot >= 0) & (slot <= count - 1))
            def _():
                attend(slot, False)

    for pair in range((heads + 1) // 2):
        low, high = spans[2 * pair]
        results = [
            acc_ref[head, :, 0:LANES] / acc_ref[head, :, LANES : 2 * LANES]
            for head in range(2 * pair, min(2 * pair + 2, heads))
        ]
        if len(results) == 2:
            lane = lax.broadcasted_iota(jnp.int32, (rows, LANES), 1)
            mixed = jnp.where(lane < HEAD_DIM, results[0], results[1])
        else:
            mixed = results[0]
        att_ref[:, low:high] = mixed[:, 0 : high - low].astype(BF16)

    small.drain(small_view, 0)
    for part in range(parts):
        frames.drain(frames_view(part), part)
    gather.finish(wo_view, 0)
    for step in range(gather.chips):
        target = gather.mate if step == 0 else gather.peer(step)
        remote(wo_ref, wog_ref.at[me], wo_sems.at[0, step, 0], wo_sems.at[1, step, 0], "grid", target).wait_send()
    for step in range(1, gather.chips):
        gather.relay(wo_view, 0, step).wait_send()
    for load in loads:
        load.wait()

    @pl.loop(0, count - 1)
    def _(step):
        for part in range(parts):

            @pl.when(has_right & (ctx - step >= 0))
            def _():
                to_right(step, part).wait_send()

            @pl.when(has_left & (ctx + step <= count - 1))
            def _():
                to_left(step, part).wait_send()


def last_kernel(
    size, count, parts, att_ref, xg_ref, affg_ref, wog_hbm, wgv_hbm, wgg_hbm, wp_hbm,
    taps_ref, out_ref,
    attg_ref, actg_ref, mid_ref, gated_ref, wo_ref, wgv_ref, wgg_ref, wp_ref,
    att_sems, act_sems, halo_sems, load_sems, wp_sems,
):
    rows, width = att_ref.shape
    step_rows = rows // parts
    ctx = lax.axis_index("ctx")
    attended = GridGather(size, att_sems)
    activated = GridGather(size, act_sems)
    me = attended.me
    has_left = ctx > 0
    has_right = ctx < count - 1

    def wp_block(index):
        if len(wp_hbm.shape) == 3:
            return wp_hbm.at[index]
        return wp_hbm.at[:, pl.ds(pl.multiple_of(index * width, LANES), width)]

    def wp_slot(index):
        return wp_ref.at[pl.ds(pl.multiple_of(index * width, HEAD_DIM), width), :]

    def send_wp(step):
        target = lax.rem(me + step, size)
        return remote(
            wp_block(target), wp_slot(me), wp_sems.at[0, step], wp_sems.at[1, step], "grid", target
        )

    def take_wp(step):
        source = lax.rem(me + size - step, size)
        return remote(
            wp_block(me), wp_slot(source), wp_sems.at[0, step], wp_sems.at[1, step], "grid", source
        )

    loads = [
        pltpu.make_async_copy(src, dst, load_sems.at[index])
        for index, (src, dst) in enumerate(
            ((wog_hbm, wo_ref), (wgv_hbm, wgv_ref), (wgg_hbm, wgg_ref), (wp_block(me), wp_slot(me)))
        )
    ]
    for load in loads:
        load.start()
    barrier = pltpu.get_barrier_semaphore()
    greeted = size - 1
    for step in range(1, size):
        pl.semaphore_signal(
            barrier, inc=1, device_id={"grid": lax.rem(me + step, size)}, device_id_type=MESH
        )

    @pl.when(has_left)
    def _():
        pl.semaphore_signal(barrier, inc=1, device_id={"ctx": ctx - 1}, device_id_type=MESH)

    @pl.when(has_right)
    def _():
        pl.semaphore_signal(barrier, inc=1, device_id={"ctx": ctx + 1}, device_id_type=MESH)

    attg_ref[me] = att_ref[...]
    inner = (ctx + count - 1) // count + (2 * count - 2 - ctx) // count
    pl.semaphore_wait(barrier, greeted + inner)

    def view(buffer, part):
        return lambda slot: buffer.at[slot, pl.ds(part * step_rows, step_rows), :]

    for part in range(parts):
        attended.start(view(attg_ref, part), part)
    for step in range(1, size):
        send_wp(step).start()

    @pl.when(jnp.logical_not(has_left))
    def _():
        gated_ref[0:PAD, :] = jnp.zeros((PAD, width), F32)

    @pl.when(jnp.logical_not(has_right))
    def _():
        gated_ref[PAD + rows : 2 * PAD + rows, :] = jnp.zeros((PAD, width), F32)

    def halo_left(index):
        return remote(
            gated_ref.at[PAD : 2 * PAD, :], gated_ref.at[PAD + rows : 2 * PAD + rows, :],
            halo_sems.at[0], halo_sems.at[1], "ctx", index,
        )

    def halo_right(index):
        return remote(
            gated_ref.at[rows : rows + PAD, :], gated_ref.at[0:PAD, :],
            halo_sems.at[2], halo_sems.at[3], "ctx", index,
        )

    attended.forward(view(attg_ref, 0), 0)
    for load in loads:
        load.wait()
    gains = [affg_ref[index, 2:3, :] for index in range(size)]
    shifts = [affg_ref[index, 3:4, :] for index in range(size)]
    for part in range(parts):
        if part + 1 < parts:
            attended.forward(view(attg_ref, part + 1), part + 1)
        attended.finish(view(attg_ref, part), part)
        span = slice(part * step_rows, (part + 1) * step_rows)
        products = project([attg_ref[index, span, :] for index in range(size)], wo_ref)
        pieces = []
        for column in range(size):
            total = products[:, column * width : (column + 1) * width]
            middle = (xg_ref[column, span, :].astype(F32) + total).astype(BF16)
            mid_ref[column, span, :] = middle
            pieces.append(middle.astype(F32))
        normed = normalize(pieces, gains, shifts)
        gate = project(normed, wgg_ref)
        value = project(normed, wgv_ref)
        gated = (value * (1.0 / (1.0 + jnp.exp(-gate)))).astype(BF16)
        gated_ref[PAD + part * step_rows : PAD + (part + 1) * step_rows, :] = gated.astype(F32)
        if part == 0:

            @pl.when(has_left)
            def _():
                halo_left(ctx - 1).start()

    @pl.when(has_right)
    def _():
        halo_right(ctx + 1).start()

    block_rows = min(32, step_rows)
    inner_parts = list(range(1, parts - 1))
    for order, part in enumerate(inner_parts + [0] + ([parts - 1] if parts > 1 else [])):
        if order == len(inner_parts):

            @pl.when(has_left)
            def _():
                halo_right(ctx - 1).wait_recv()

            @pl.when(has_right)
            def _():
                halo_left(ctx + 1).wait_recv()

        @pl.loop(0, step_rows // block_rows)
        def _(block):
            base = pl.multiple_of(part * step_rows + block * block_rows, block_rows)
            window = gated_ref[pl.ds(base, block_rows + 2 * PAD), :]
            total = jnp.zeros((block_rows, width), F32)
            for tap in range(KERNEL):
                low = tap + PAD - HALF
                total = total + taps_ref[tap : tap + 1, :] * window[low : low + block_rows, :]
            scaled = total * affg_ref[me, 4:5, :] + affg_ref[me, 5:6, :]
            result = scaled / (1.0 + jnp.exp(-scaled))
            actg_ref[me, pl.ds(base, block_rows), :] = result.astype(BF16)

        activated.start(view(actg_ref, part), part)

    sequence = inner_parts + [0] + ([parts - 1] if parts > 1 else [])
    activated.forward(view(actg_ref, sequence[0]), sequence[0])
    for step in range(1, size):
        take_wp(step).wait_recv()
    for order, part in enumerate(sequence):
        if order + 1 < parts:
            activated.forward(view(actg_ref, sequence[order + 1]), sequence[order + 1])
        activated.finish(view(actg_ref, part), part)
        span = slice(part * step_rows, (part + 1) * step_rows)
        total = mid_ref[me, span, :].astype(F32)
        total = total + project([actg_ref[index, span, :] for index in range(size)], wp_ref)
        out_ref[span, :] = total.astype(BF16)

    for part in range(parts):
        attended.drain(view(attg_ref, part), part)
        activated.drain(view(actg_ref, part), part)
    for step in range(1, size):
        send_wp(step).wait_send()

    @pl.when(has_left)
    def _():
        halo_left(ctx - 1).wait_send()

    @pl.when(has_right)
    def _():
        halo_right(ctx + 1).wait_send()


def params(number):
    return pltpu.CompilerParams(
        collective_id=number, has_side_effects=True, vmem_limit_bytes=VMEM_LIMIT
    )


def on_device(
    frames_in,
    norm1_gain,
    norm1_bias,
    w_query,
    w_key,
    w_value,
    w_out,
    norm2_gain,
    norm2_bias,
    w_glu_value,
    w_glu_gate,
    depth_kernel,
    bn_scale,
    bn_shift,
    w_proj,
):
    size = lax.axis_size("grid")
    count = lax.axis_size("ctx")
    rows, width = frames_in.shape
    full = width * size
    heads = width // HEAD_DIM
    vmem = pl.BlockSpec(memory_space=pltpu.VMEM)
    anywhere = pl.BlockSpec(memory_space=pl.ANY)
    dma = pltpu.SemaphoreType.DMA
    parts = 4

    def shape(dims, dtype=BF16):
        return jax.ShapeDtypeStruct(dims, dtype)

    wp_blocks = w_proj
    if width % LANES:
        wp_blocks = jnp.transpose(w_proj.reshape(width, size, width), (1, 0, 2))
    weight = pltpu.VMEM((full, width), BF16)
    attended, xg, affg, wo_all = pl.pallas_call(
        lambda *refs: attend_kernel(size, count, parts, *refs),
        out_shape=(
            shape((rows, width)),
            shape((size, rows, width)),
            shape((size, 8, width), F32),
            shape((size, width, full)),
        ),
        in_specs=[vmem] * 7 + [anywhere] * 4,
        out_specs=(vmem, vmem, vmem, anywhere),
        scratch_shapes=[
            weight,
            weight,
            weight,
            pltpu.VMEM((rows, width), BF16),
            pltpu.VMEM((count, 2, rows, width), BF16),
            pltpu.VMEM((heads, rows, LANES), BF16),
            pltpu.VMEM((heads, rows, LANES), F32),
            pltpu.VMEM((heads, rows, 2 * LANES), F32),
            gather_sems(size, parts),
            gather_sems(size, 1),
            dma((2, count, parts)),
            dma((2, count, parts)),
            gather_sems(size, 1),
            dma((1,)),
            dma((3,)),
        ],
        compiler_params=params(1),
        name="attend_ring",
    )(
        frames_in, norm1_gain, norm1_bias, norm2_gain, norm2_bias, bn_scale, bn_shift,
        w_query, w_key, w_value, w_out,
    )

    return pl.pallas_call(
        lambda *refs: last_kernel(size, count, parts, *refs),
        out_shape=shape((rows, width)),
        in_specs=[vmem, vmem, vmem] + [anywhere] * 4 + [vmem],
        out_specs=vmem,
        scratch_shapes=[
            pltpu.VMEM((size, rows, width), BF16),
            pltpu.VMEM((size, rows, width), BF16),
            pltpu.VMEM((size, rows, width), BF16),
            pltpu.VMEM((rows + 2 * PAD, width), F32),
            pltpu.VMEM((full, full), BF16),
            pltpu.VMEM((full, width), BF16),
            pltpu.VMEM((full, width), BF16),
            pltpu.VMEM((full, width), BF16),
            gather_sems(size, parts),
            gather_sems(size, parts),
            dma((4,)),
            dma((4,)),
            dma((2, size)),
        ],
        compiler_params=params(2),
        name="convolve_project",
    )(
        attended, xg, affg, wo_all.reshape(full, full), w_glu_value, w_glu_gate,
        wp_blocks, depth_kernel,
    )


def solution(mesh):
    return jax.shard_map(
        on_device,
        mesh=mesh,
        in_specs=(
            P(("parts", "ctx"), "grid"),
            P("grid"),
            P("grid"),
            P(None, "grid"),
            P(None, "grid"),
            P(None, "grid"),
            P("grid", None),
            P("grid"),
            P("grid"),
            P(None, "grid"),
            P(None, "grid"),
            P(None, "grid"),
            P("grid"),
            P("grid"),
            P("grid", None),
        ),
        out_specs=P(("parts", "ctx"), "grid"),
        check_vma=False,
    )
```
